256 devices in a mesh: gy: 16 (over z, core), gz: 16 (over y, x).
Axes of the slice: x: 4, y: 4, z: 8, core: 2. Of those that a mesh axis runs over, the one named last changes fastest.
Arguments:
- latent: float32 [32, 64, 4096], P('gz', 'gy'), may hold values from -2.5 to 2.5
- event_counts: int32 [32, 64, 4096], P('gz', 'gy'), may hold values from 0 to 7
- survey_mask: int32 [32, 64, 4096], P('gz', 'gy'), may hold values from 0 to 1, as said below
- class_ids: int32 [32, 64, 4096], P('gz', 'gy'), may hold values from 0 to 15
- class_table: float32 [4, 16], replicated, may hold values from 0.5 to 2
Outputs:
- newton_step: float32 [32, 64, 4096], P('gz', 'gy')
The draws below stay inside these ranges and needn't reach their ends.
Inputs may be any that keep to these rules, and one draw needn't show every extreme that they name: `survey_mask`: 1 where the cell lies inside the survey, else 0.
All inputs are finite; a program needn't handle non-finite values.
Results may differ from the reference program's by a relative error of at most 0.0001.
Values sent between devices are 32-bit elements; how exact they have to be, the bound alone decides.
A program may use at most 64 MiB of HBM per device.

```python
import math
import jax
import jax.numpy as jnp
from jax import lax

NX = 4096
ITERS = 3
NCLASS = 16
NY = 64
NZ = 32


def draw_latent(key, part):
    shape = (NZ, NY, NX)
    row_pos = (jnp.arange(NY, dtype=jnp.float32) / max(NY - 1, 1))[None, :, None]
    column_pos = (jnp.arange(NX, dtype=jnp.float32) / max(NX - 1, 1))[None, None, :]
    spread = 0.1 * jnp.power(10.0, row_pos) * jnp.power(3.0, column_pos - 1.0)
    noise = jnp.clip(jax.random.normal(key, shape, jnp.float32), -2.5, 2.5)
    return (spread * noise).astype(jnp.float32)


def draw_survey_mask(key, part):
    shape = (NZ, NY, NX)
    row_index = jnp.arange(NY, dtype=jnp.int32)[None, :, None]
    tickets = jax.random.randint(key, shape, 0, 10 * NY, dtype=jnp.int32)
    return (tickets < 2 * NY + 7 * row_index).astype(jnp.int32)


def plant(drawn, own_key, least, high):
    dims = drawn.shape
    place = [jax.random.randint(jax.random.fold_in(own_key, axis), (), 0, dims[axis]) for axis in range(len(dims))]
    drawn = drawn.at[tuple(place)].set(least)
    longest = dims.index(max(dims))
    place[longest] = (place[longest] + 1) % dims[longest]
    return drawn.at[tuple(place)].set(high)


def setup_inputs(seed: int = 0) -> dict:
    seeds = jax.random.split(jax.random.key(seed), 6)
    latent = draw_latent(jax.random.fold_in(seeds[5], 71), 0)
    event_counts = plant(jax.random.randint(seeds[1], (NZ, NY, NX), 0, 8), jax.random.fold_in(seeds[1], 1), 0, 7).astype(jnp.int32)
    survey_mask = draw_survey_mask(jax.random.fold_in(seeds[5], 71), 0)
    class_ids = plant(jax.random.randint(seeds[3], (NZ, NY, NX), 0, NCLASS), jax.random.fold_in(seeds[3], 1), 0, NCLASS - 1).astype(jnp.int32)
    class_table = jnp.clip(jnp.exp(jax.random.uniform(seeds[4], (4, NCLASS), jnp.float32, math.log(0.5), math.log(2.0))), 0.5, 2.0)
    return dict(latent=latent, event_counts=event_counts, survey_mask=survey_mask, class_ids=class_ids, class_table=class_table)


CELL_SCALES = (0.05, 4.0, 400.0, 1.0)

def shift_prev(values, line_axis):
    length = values.shape[line_axis]
    kept_part = lax.slice_in_dim(values, 0, length - 1, axis=line_axis)
    edge_fill = jnp.zeros_like(lax.slice_in_dim(values, 0, 1, axis=line_axis))
    return jnp.concatenate([edge_fill, kept_part], axis=line_axis)

def shift_next(values, line_axis):
    length = values.shape[line_axis]
    kept_part = lax.slice_in_dim(values, 1, length, axis=line_axis)
    edge_fill = jnp.zeros_like(lax.slice_in_dim(values, 0, 1, axis=line_axis))
    return jnp.concatenate([kept_part, edge_fill], axis=line_axis)

def face_bands(conduct, line_axis):
    length = conduct.shape[line_axis]
    upper_cells = lax.slice_in_dim(conduct, 1, length, axis=line_axis)
    lower_cells = lax.slice_in_dim(conduct, 0, length - 1, axis=line_axis)
    faces = 0.5 * (upper_cells + lower_cells)
    zero_face = jnp.zeros_like(lax.slice_in_dim(conduct, 0, 1, axis=line_axis))
    return (jnp.concatenate([zero_face, faces], axis=line_axis), jnp.concatenate([faces, zero_face], axis=line_axis))

def stencil(values, center, bands):
    x_lower, x_upper, y_lower, y_upper, z_lower, z_upper = bands
    result = center * values - x_lower * shift_prev(values, 2) - x_upper * shift_next(values, 2)
    result = result - y_lower * shift_prev(values, 1) - y_upper * shift_next(values, 1)
    result = result - z_lower * shift_prev(values, 0) - z_upper * shift_next(values, 0)
    return result

def solve_lines(lower_band, diagonal, upper_band, right_side, line_axis):
    moved = [jnp.moveaxis(item, line_axis, -1) for item in (lower_band, diagonal, upper_band, right_side)]
    solved = lax.linalg.tridiagonal_solve(moved[0], moved[1], moved[2], moved[3][..., None])[..., 0]
    return jnp.moveaxis(solved, -1, line_axis)

def reference(latent, event_counts, survey_mask, class_ids, class_table):
    scaled = class_table * jnp.array(CELL_SCALES, jnp.float32)[:, None]
    coeffs = scaled[:, class_ids]
    reaction = coeffs[0]
    x_lower, x_upper = face_bands(coeffs[1], 2)
    y_lower, y_upper = face_bands(coeffs[2], 1)
    z_lower, z_upper = face_bands(coeffs[3], 0)
    bands = (x_lower, x_upper, y_lower, y_upper, z_lower, z_upper)
    center_q = reaction + x_lower + x_upper + y_lower + y_upper + z_lower + z_upper
    growth = jnp.exp(latent)
    observed = survey_mask.astype(jnp.float32)
    intensity = observed * growth
    rhs = observed * (event_counts.astype(jnp.float32) - growth) - stencil(latent, center_q, bands)
    center_h = center_q + intensity
    half_diagonal = 0.5 * (reaction + intensity + (z_lower + z_upper))
    x_diagonal = half_diagonal + x_lower + x_upper
    y_diagonal = half_diagonal + y_lower + y_upper

    def precondition(residual):
        along_x = solve_lines(-x_lower, x_diagonal, -x_upper, residual, 2)
        along_y = solve_lines(-y_lower, y_diagonal, -y_upper, residual, 1)
        return along_x + along_y
    newton = jnp.zeros_like(latent)
    residual = rhs
    search = precondition(residual)
    direction = search
    product = jnp.sum(residual * search)
    for iteration in range(ITERS):
        applied = stencil(direction, center_h, bands)
        step_size = product / jnp.sum(direction * applied)
        newton = newton + step_size * direction
        if iteration + 1 < ITERS:
            residual = residual - step_size * applied
            search = precondition(residual)
            following = jnp.sum(residual * search)
            direction = search + following / product * direction
            product = following
    return newton
```

```python
import functools
import jax
import jax.numpy as jnp
from jax import lax
from jax.experimental import pallas as pl
from jax.experimental.pallas import tpu as pltpu
from jax.sharding import PartitionSpec as P

CELL_SCALES = (0.05, 4.0, 400.0, 1.0)
LANES = 128
COEFS = (
    "e0", "eu1", "eu2", "eu3", "ed1", "ed2",
    "g0", "gu1", "gu2", "gd1", "gd2", "pp", "qq",
    "px", "py", "xl", "xu", "yl", "yu", "za", "zb",
)
VECS = ("r", "u0", "w0", "q0", "z0", "u1", "w1", "s1", "ax", "ay", "part")


def up(values, amount):
    return pltpu.roll(values, amount, 0)


def down(values, amount):
    return pltpu.roll(values, 8 - amount, 0)


def before(values, amount):
    return pltpu.roll(values, amount, 1)


def after(values, amount):
    return pltpu.roll(values, values.shape[1] - amount, 1)


def far_first(count):
    order = sorted(range(1, count), key=lambda o: -min(o, count - o))
    return order


def kernel(
    n, m, width,
    lat_h, cnt_h, msk_h, cls_h, tbl,
    out,
    lat_v, cnt_v, msk_v, cls_v, in_sem,
    y0s, y0r, z0s, z0r, h_ss, h_rs,
    fs, fr, f_ss, f_rs,
    as_, ar, a_ss, a_rs,
    bs, br, b_ss, b_rs,
    ys, yr, zs, zr, k_ss, k_rs,
    p1s, p1r, p1_ss, p1_rs,
    p2s, p2r, p2_ss, p2_rs,
    wb, wa, xinv, coef, vec, sol, sinv, smul,
):
    gy = lax.axis_index("gy")
    gz = lax.axis_index("gz")
    tiles = width // LANES

    def peer(axis, offset):
        if axis == "gy":
            return lax.rem(gy + offset, n)
        return lax.rem(gz + offset, m)

    loads = []
    for index, (src, dst) in enumerate(((cls_h, cls_v), (lat_h, lat_v), (msk_h, msk_v), (cnt_h, cnt_v))):
        copy = pltpu.make_async_copy(src, dst, in_sem.at[index])
        copy.start()
        loads.append(copy)

    barrier = pltpu.get_barrier_semaphore()
    for axis, count in (("gy", n), ("gz", m)):
        for offset in far_first(count):
            pl.semaphore_signal(
                barrier, inc=1, device_id={axis: peer(axis, offset)},
                device_id_type=pl.DeviceIdType.MESH,
            )

    pending = []

    def send(src, dst, send_sem, recv_sem, axis, target):
        copy = pltpu.make_async_remote_copy(
            src_ref=src, dst_ref=dst, send_sem=send_sem, recv_sem=recv_sem,
            device_id={axis: target}, device_id_type=pl.DeviceIdType.MESH,
        )
        copy.start()
        pending.append(copy)
        return copy

    sub = lax.broadcasted_iota(jnp.int32, (8, width), 0)
    row = lax.rem(sub, 4)
    is0 = row == 0
    is1 = row == 1
    is2 = row == 2
    is3 = row == 3
    low = sub < 4
    sub1 = lax.broadcasted_iota(jnp.int32, (8, LANES), 0)
    row1 = lax.rem(sub1, 4)
    edge1 = (row1 == 0) | (row1 == 3)
    odd1 = lax.rem(sub1, 2) == 1

    def merge(ref):
        return jnp.concatenate([ref[0], ref[1]], axis=0)

    def spread(values, source):
        result = values
        for target in range(4):
            if target > source:
                result = jnp.where(row == target, up(values, target - source), result)
            if target < source:
                result = jnp.where(row == target, down(values, source - target), result)
        return result

    def pack(values, chunk):
        first = values[:, 2 * chunk * LANES : (2 * chunk + 1) * LANES]
        second = values[:, (2 * chunk + 1) * LANES : (2 * chunk + 2) * LANES]
        return jnp.where(edge1, first, up(second, 2))

    def rows_out(values, ref):
        ref[0] = jnp.concatenate([values[0:1], values[4:5]], axis=0)
        ref[1] = jnp.concatenate([values[3:4], values[7:8]], axis=0)

    def rows_in(from_prev, from_next):
        a = from_prev[...]
        b = from_next[...]
        return jnp.concatenate(
            [a[0:1], a[0:1], b[0:1], b[0:1], a[1:2], a[1:2], b[1:2], b[1:2]], axis=0
        )

    def planes_out(values, ref):
        ref[0] = values[0:4]
        ref[1] = values[4:8]

    def halo(src, dst, sems, axis, base):
        count = n if axis == "gy" else m
        back = send(src.at[0], dst.at[1], sems[0].at[base], sems[1].at[base], axis, peer(axis, count - 1))
        ahead = send(src.at[1], dst.at[0], sems[0].at[base + 1], sems[1].at[base + 1], axis, peer(axis, 1))
        return back, ahead

    loads[0].wait()
    classes = merge(cls_v)
    bits = [(classes & (1 << k)) != 0 for k in range(4)]

    def lookup(kind):
        scaled = [tbl[kind, c] * CELL_SCALES[kind] for c in range(16)]
        level = [
            jnp.where(bits[0], scaled[2 * c + 1], scaled[2 * c]) for c in range(8)
        ]
        level = [jnp.where(bits[1], level[2 * c + 1], level[2 * c]) for c in range(4)]
        level = [jnp.where(bits[2], level[2 * c + 1], level[2 * c]) for c in range(2)]
        return jnp.where(bits[3], level[1], level[0])

    cond_y = lookup(2)
    cond_z = lookup(3)
    rows_out(cond_y, y0s.at[0])
    planes_out(cond_z, z0s.at[0])
    loads[1].wait()
    latent = merge(lat_v)
    rows_out(latent, y0s.at[1])
    planes_out(latent, z0s.at[1])

    pl.semaphore_wait(barrier, (n - 1) + (m - 1))

    start = []
    start += halo(z0s.at[0], z0r.at[0], (h_ss, h_rs), "gz", 0)
    start += halo(y0s.at[0], y0r.at[0], (h_ss, h_rs), "gy", 2)
    start += halo(z0s.at[1], z0r.at[1], (h_ss, h_rs), "gz", 4)
    start += halo(y0s.at[1], y0r.at[1], (h_ss, h_rs), "gy", 6)

    reaction = lookup(0)
    cond_x = lookup(1)
    column = lax.broadcasted_iota(jnp.int32, (8, width), 1)
    xl = jnp.where(column >= 1, 0.5 * (cond_x + before(cond_x, 1)), 0.0)
    xu = jnp.where(column < width - 1, 0.5 * (cond_x + after(cond_x, 1)), 0.0)
    loads[2].wait()
    loads[3].wait()
    observed = merge(msk_v).astype(jnp.float32)
    counts = merge(cnt_v).astype(jnp.float32)
    growth = jnp.exp(latent)
    intensity = observed * growth

    for copy in start[:4]:
        copy.wait_recv()
    top = gy == 0
    bottom = gy == n - 1
    halo_y = rows_in(y0r.at[0, 0], y0r.at[0, 1])
    prev_y = jnp.where(is0, halo_y, up(cond_y, 1))
    next_y = jnp.where(is3, halo_y, down(cond_y, 1))
    yl = 0.5 * (cond_y + prev_y)
    yu = 0.5 * (cond_y + next_y)
    yl = jnp.where(is0 & top, 0.0, yl)
    yu = jnp.where(is3 & bottom, 0.0, yu)
    halo_z = merge(z0r.at[0])
    inner = 0.5 * (cond_z + up(cond_z, 4))
    outer = 0.5 * (cond_z + halo_z)
    closed = jnp.where(low, jnp.where(gz == 0, 1, 0), jnp.where(gz == m - 1, 1, 0)) == 1
    outer = jnp.where(closed, 0.0, outer)
    zl = jnp.where(low, outer, inner)
    zu = jnp.where(low, inner, outer)
    half = 0.5 * (reaction + intensity + (zl + zu))
    px = half + xl + xu
    py = half + yl + yu

    def put(name, values):
        coef[COEFS.index(name)] = values

    def get(name):
        return coef[COEFS.index(name)]

    def vput(name, values):
        vec[VECS.index(name)] = values

    def vget(name):
        return vec[VECS.index(name)]

    for name, values in (
        ("px", px), ("py", py), ("xl", xl), ("xu", xu), ("yl", yl), ("yu", yu),
        ("za", inner), ("zb", outer),
    ):
        put(name, values)

    d0 = spread(py, 0)
    d1 = spread(py, 1)
    d2 = spread(py, 2)
    a1 = spread(yl, 1)
    a2 = spread(yl, 2)
    l0 = spread(yl, 0)
    l3 = spread(yl, 3)
    minor0 = d1 * d2 - a2 * a2
    inv_det = 1.0 / (d0 * minor0 - a1 * a1 * d2)
    i00 = minor0 * inv_det
    i01 = a1 * d2 * inv_det
    i02 = a1 * a2 * inv_det
    i11 = d0 * d2 * inv_det
    i12 = a2 * d0 * inv_det
    i22 = (d0 * d1 - a1 * a1) * inv_det
    put("e0", jnp.where(is3, 1.0, l0 * i00))
    put("eu1", jnp.where(is3, l3 * i22, 0.0))
    put("eu2", jnp.where(is3, l3 * i12, 0.0))
    put("eu3", jnp.where(is3, l3 * i02, 0.0))
    put("ed1", jnp.where(is0, l0 * i01, 0.0))
    put("ed2", jnp.where(is0, l0 * i02, 0.0))
    put("g0", jnp.where(is0, i00, jnp.where(is1, i11, jnp.where(is2, i22, 0.0))))
    put("gd1", jnp.where(is0, i01, jnp.where(is1, i12, 0.0)))
    put("gd2", jnp.where(is0, i02, 0.0))
    put("gu1", jnp.where(is1, i01, jnp.where(is2, i12, 0.0)))
    put("gu2", jnp.where(is2, i02, 0.0))
    put("pp", l0 * jnp.where(is0, i00, jnp.where(is1, i01, jnp.where(is2, i02, 0.0))))
    put("qq", jnp.where(is3, 1.0, l3 * jnp.where(is0, i02, jnp.where(is1, i12, i22))))
    main = jnp.where(is3, py - l3 * l3 * i22, -(l0 * l0 * i00))
    link = jnp.where(is3, l3 * i02 * l0, 0.0)
    for chunk in range(n):
        fs[chunk, 0] = pack(main, chunk)
        fs[chunk, 1] = pack(link, chunk)

    def exchange(src, dst, send_sems, recv_sems):
        copies = []
        dst[gy] = src[gy]
        for offset in far_first(n):
            target = peer("gy", offset)
            copies.append(
                send(src.at[target], dst.at[gy], send_sems.at[offset], recv_sems.at[offset], "gy", target)
            )
        return copies

    factor_copies = exchange(fs, fr, f_ss, f_rs)

    for copy in start[4:]:
        copy.wait_recv()
    halo_y = rows_in(y0r.at[1, 0], y0r.at[1, 1])
    halo_z = merge(z0r.at[1])
    center_q = reaction + xl + xu + yl + yu + zl + zu
    applied = (
        center_q * latent - xl * before(latent, 1) - xu * after(latent, 1)
        - yl * jnp.where(is0, halo_y, up(latent, 1))
        - yu * jnp.where(is3, halo_y, down(latent, 1))
        - inner * up(latent, 4) - outer * halo_z
    )
    rhs = observed * (counts - growth) - applied
    vput("r", rhs)

    def forward(k, values):
        gathered = (
            get("e0") * values
            + get("eu1") * up(values, 1) + get("eu2") * up(values, 2) + get("eu3") * up(values, 3)
            + get("ed1") * down(values, 1) + get("ed2") * down(values, 2)
        )
        for chunk in range(n):
            as_[k, chunk] = pack(gathered, chunk)
        return exchange(as_.at[k], ar.at[k], a_ss.at[k], a_rs.at[k])

    def x_factors():
        diagonal = get("px")
        band = get("xu")
        stride = 1
        level = 0
        while stride < width:
            inverse = 1.0 / diagonal
            scaled = band * inverse
            ahead = band * after(inverse, stride)
            wb[level] = before(scaled, stride)
            wa[level] = ahead
            diagonal = diagonal - before(scaled * band, stride) - ahead * band
            band = ahead * after(band, stride)
            stride = stride * 2
            level = level + 1
        xinv[...] = 1.0 / diagonal

    def solve_x(values):
        stride = 1
        level = 0
        while stride < width:
            values = values + wb[level] * before(values, stride) + wa[level] * after(values, stride)
            stride = stride * 2
            level = level + 1
        return values * xinv[...]

    def line_factors():
        for copy in factor_copies:
            copy.wait_recv()
        inverse = None
        for i in range(n):
            diagonal = fr[i, 0]
            if i + 1 < n:
                diagonal = diagonal + up(fr[i + 1, 0], 3)
            diagonal = jnp.where(odd1, diagonal, 1.0)
            if i > 0:
                off = jnp.where(odd1, fr[i, 1], 0.0)
                scale = off * inverse
                smul[i] = scale
                diagonal = diagonal - scale * off
            inverse = 1.0 / diagonal
            sinv[i] = inverse

    def solve_separators(k, copies):
        for copy in copies:
            copy.wait_recv()
        carried = None
        for i in range(n):
            right = ar[k, i]
            if i + 1 < n:
                right = right + up(ar[k, i + 1], 3)
            carried = right if i == 0 else right + smul[i] * carried
            sol[i] = carried
        solved = None
        for i in range(n - 1, -1, -1):
            solved = sol[i] * sinv[i] if i == n - 1 else sol[i] * sinv[i] + smul[i + 1] * solved
            sol[i] = solved
        for i in range(n):
            below = sol[i - 1] if i > 0 else jnp.zeros((8, LANES), jnp.float32)
            bs[k, i] = jnp.where(odd1, sol[i], up(below, 5))
        return exchange(bs.at[k], br.at[k], b_ss.at[k], b_rs.at[k])

    def unpack(k):
        parts = []
        for chunk in range(n):
            block = br[k, chunk]
            parts += [block, up(block, 6)]
        return jnp.concatenate(parts, axis=1)

    def apply_pair(k, name, middle, extra=None):
        values = vget(name)
        fwd = forward(k, values)
        if k == 0:
            x_factors()
        if extra is not None:
            extra()
        along_x = solve_x(vget(name))
        vput("ax", along_x)
        rows_out(along_x, ys.at[k])
        y_halo = halo(ys.at[k], yr.at[k], (k_ss.at[k], k_rs.at[k]), "gy", 0)
        if k == 0:
            line_factors()
        values = vget(name)
        vput(
            "ay",
            get("g0") * values + get("gu1") * up(values, 1) + get("gu2") * up(values, 2)
            + get("gd1") * down(values, 1) + get("gd2") * down(values, 2),
        )
        back = solve_separators(k, fwd)
        if middle is not None:
            middle()
        for copy in y_halo:
            copy.wait_recv()
        along_x = vget("ax")
        edge = rows_in(yr.at[k, 0], yr.at[k, 1])
        vput(
            "part",
            2.0 * vget(name) + get("py") * along_x
            - get("yl") * jnp.where(is0, edge, up(along_x, 1))
            - get("yu") * jnp.where(is3, edge, down(along_x, 1)),
        )
        for copy in back:
            copy.wait_recv()
        ends = unpack(k)
        along_y = vget("ay") + get("pp") * spread(ends, 0) + get("qq") * spread(ends, 3)
        total = vget("ax") + along_y
        planes_out(total, zs.at[k])
        z_halo = halo(zs.at[k], zr.at[k], (k_ss.at[k], k_rs.at[k]), "gz", 2)
        image = (
            vget("part") + get("px") * along_y
            - get("xl") * before(along_y, 1) - get("xu") * after(along_y, 1)
            - get("za") * up(total, 4)
        )
        for copy in z_halo:
            copy.wait_recv()
        image = image - get("zb") * merge(zr.at[k])
        return total, image

    def fold(first, second):
        product = first * second
        acc = product[:, 0:LANES]
        for t in range(1, tiles):
            acc = acc + product[:, t * LANES : (t + 1) * LANES]
        return jnp.sum(jnp.sum(acc, axis=0, keepdims=True), axis=1, keepdims=True)

    lane = lax.broadcasted_iota(jnp.int32, (1, LANES), 1)

    def reduce_start(k, sums):
        packed = jnp.zeros((1, LANES), jnp.float32)
        for index, value in enumerate(sums):
            packed = jnp.where(lane == index, value, packed)
        p1s[k] = packed
        p1r[k, gy] = packed
        copies = []
        for offset in far_first(n):
            copies.append(
                send(p1s.at[k], p1r.at[k, gy], p1_ss.at[k, offset], p1_rs.at[k, offset], "gy", peer("gy", offset))
            )
        return copies

    def reduce_middle(k, copies):
        for copy in copies:
            copy.wait_recv()
        total = p1r[k, 0]
        for i in range(1, n):
            total = total + p1r[k, i]
        p2s[k] = total
        p2r[k, gz] = total
        result = []
        for offset in far_first(m):
            result.append(
                send(p2s.at[k], p2r.at[k, gz], p2_ss.at[k, offset], p2_rs.at[k, offset], "gz", peer("gz", offset))
            )
        return result

    def reduce_end(k, copies, count):
        for copy in copies:
            copy.wait_recv()
        total = p2r[k, 0]
        for i in range(1, m):
            total = total + p2r[k, i]
        return [total[:, index : index + 1] for index in range(count)]

    box = {}

    u0, w0 = apply_pair(0, "r", None)
    vput("u0", u0)
    vput("w0", w0)

    def start0():
        box["c"] = reduce_start(0, (fold(vget("r"), vget("u0")), fold(vget("u0"), vget("w0"))))

    def middle0():
        box["c"] = reduce_middle(0, box["c"])

    q0, z0 = apply_pair(1, "w0", middle0, start0)
    vput("q0", q0)
    vput("z0", z0)
    g0, e0 = reduce_end(0, box["c"], 2)
    alpha0 = g0 / e0
    r1 = vget("r") - alpha0 * vget("w0")
    u1 = vget("u0") - alpha0 * vget("q0")
    w1 = vget("w0") - alpha0 * vget("z0")
    vput("r", r1)
    vput("u1", u1)
    vput("w1", w1)

    def start1():
        box["c"] = reduce_start(
            1,
            (
                fold(vget("r"), vget("u1")),
                fold(vget("u1"), vget("w1")),
                fold(vget("u1"), vget("w0")),
            ),
        )

    def middle1():
        box["c"] = reduce_middle(1, box["c"])

    q1, z1 = apply_pair(2, "w1", middle1, start1)
    g1, uw1, c1 = reduce_end(1, box["c"], 3)
    beta1 = g1 / g0
    e1 = uw1 + 2.0 * beta1 * c1 + beta1 * beta1 * e0
    alpha1 = g1 / e1
    s1 = vget("w1") + beta1 * vget("w0")
    r2 = vget("r") - alpha1 * s1
    u2 = vget("u1") - alpha1 * (q1 + beta1 * vget("q0"))
    w2 = vget("w1") - alpha1 * (z1 + beta1 * vget("z0"))
    last = reduce_middle(2, reduce_start(2, (fold(r2, u2), fold(u2, w2), fold(u2, s1))))
    dir1 = vget("u1") + beta1 * vget("u0")
    done = alpha0 * vget("u0") + alpha1 * dir1
    g2, uw2, c2 = reduce_end(2, last, 3)
    beta2 = g2 / g1
    e2 = uw2 + 2.0 * beta2 * c2 + beta2 * beta2 * e1
    alpha2 = g2 / e2
    result = done + alpha2 * (u2 + beta2 * dir1)
    out[0] = result[0:4]
    out[1] = result[4:8]
    for copy in pending:
        copy.wait_send()


def shards(latent, event_counts, survey_mask, class_ids, class_table):
    planes, rows, width = latent.shape
    n = lax.axis_size("gy")
    m = lax.axis_size("gz")
    assert planes == 2 and rows == 4 and width == n * 2 * LANES
    levels = 0
    while (1 << levels) < width:
        levels = levels + 1
    f32 = jnp.float32
    dma = pltpu.SemaphoreType.DMA
    vmem = pltpu.VMEM
    block = (2, 4, width)
    scratch = [
        vmem(block, f32), vmem(block, jnp.int32), vmem(block, jnp.int32), vmem(block, jnp.int32), dma((4,)),
        vmem((2, 2, 2, width), f32), vmem((2, 2, 2, width), f32),
        vmem((2, 2, 4, width), f32), vmem((2, 2, 4, width), f32), dma((8,)), dma((8,)),
        vmem((n, 2, 8, LANES), f32), vmem((n, 2, 8, LANES), f32), dma((n,)), dma((n,)),
        vmem((3, n, 8, LANES), f32), vmem((3, n, 8, LANES), f32), dma((3, n)), dma((3, n)),
        vmem((3, n, 8, LANES), f32), vmem((3, n, 8, LANES), f32), dma((3, n)), dma((3, n)),
        vmem((3, 2, 2, width), f32), vmem((3, 2, 2, width), f32),
        vmem((3, 2, 4, width), f32), vmem((3, 2, 4, width), f32), dma((3, 4)), dma((3, 4)),
        vmem((3, 1, LANES), f32), vmem((3, n, 1, LANES), f32), dma((3, n)), dma((3, n)),
        vmem((3, 1, LANES), f32), vmem((3, m, 1, LANES), f32), dma((3, m)), dma((3, m)),
        vmem((levels, 8, width), f32), vmem((levels, 8, width), f32), vmem((8, width), f32),
        vmem((len(COEFS), 8, width), f32), vmem((len(VECS), 8, width), f32),
        vmem((n, 8, LANES), f32), vmem((n, 8, LANES), f32), vmem((n, 8, LANES), f32),
    ]
    anywhere = pl.BlockSpec(memory_space=pl.ANY)
    return pl.pallas_call(
        functools.partial(kernel, n, m, width),
        out_shape=jax.ShapeDtypeStruct(block, f32),
        in_specs=[anywhere] * 4 + [pl.BlockSpec(memory_space=pltpu.SMEM)],
        out_specs=pl.BlockSpec(memory_space=pltpu.VMEM),
        scratch_shapes=scratch,
        compiler_params=pltpu.CompilerParams(collective_id=0, has_side_effects=True),
        name="newton",
    )(latent, event_counts, survey_mask, class_ids, class_table)


def solution(mesh):
    placed = (
        P("gz", "gy", None),
        P("gz", "gy", None),
        P("gz", "gy", None),
        P("gz", "gy", None),
        P(),
    )
    return jax.shard_map(
        shards, mesh=mesh, in_specs=placed, out_specs=P("gz", "gy", None), check_vma=False
    )
```

```python
import functools
import jax
import jax.numpy as jnp
from jax import lax
from jax.experimental import pallas as pl
from jax.experimental.pallas import tpu as pltpu
from jax.sharding import PartitionSpec as P

CELL_SCALES = (0.05, 4.0, 400.0, 1.0)
LANES = 128
ITERS = 3
COEFS = (
    "e0", "eu1", "eu2", "eu3", "ed1", "ed2",
    "g0", "gu1", "gu2", "gd1", "gd2", "pp", "qq",
    "px", "py", "xl", "xu", "yl", "yu", "za", "zb",
)
VECS = ("r", "u0", "w0", "q0", "z0", "u1", "w1", "s1", "ax", "ay", "part")


def up(values, amount):
    return pltpu.roll(values, amount, 0)


def down(values, amount):
    return pltpu.roll(values, 8 - amount, 0)


def before(values, amount):
    return pltpu.roll(values, amount, 1)


def after(values, amount):
    return pltpu.roll(values, values.shape[1] - amount, 1)


def far_first(count):
    order = sorted(range(1, count), key=lambda o: -min(o, count - o))
    return order


def kernel(
    n, m, width,
    lat_h, cnt_h, msk_h, cls_h, tbl_h,
    out,
    lat_v, cnt_v, msk_v, cls_v, tbl, in_sem, ready,
    y0s, y0r, z0s, z0r, h_ss, h_rs,
    fs, fr, f_sem,
    as_, ar, a_sem,
    bs, br, b_sem,
    ys, yr, zs, zr, k_ss, k_rs,
    p1s, p1r, p1_sem,
    p2s, p2r, p2_sem,
    wb, wa, xinv, coef, vec, sol, sinv, smul,
):
    gy = lax.axis_index("gy")
    gz = lax.axis_index("gz")
    tiles = width // LANES

    def peer(axis, offset):
        if axis == "gy":
            return lax.rem(gy + offset, n)
        return lax.rem(gz + offset, m)

    mesh_id = pl.DeviceIdType.MESH

    def signal(sem, axis, offset):
        pl.semaphore_signal(sem, inc=1, device_id={axis: peer(axis, offset)}, device_id_type=mesh_id)

    barrier = pltpu.get_barrier_semaphore()
    for axis, count in (("gz", m), ("gy", n)):
        signal(barrier, axis, 1)
        signal(barrier, axis, count - 1)

    loads = []
    for index, (src, dst) in enumerate(
        ((cls_h, cls_v), (tbl_h, tbl), (lat_h, lat_v), (msk_h, msk_v), (cnt_h, cnt_v))
    ):
        copy = pltpu.make_async_copy(src, dst, in_sem.at[index])
        copy.start()
        loads.append(copy)

    rounds = []
    for position, (axis, count) in enumerate((("gy", n), ("gz", m))):
        reach = 1
        step = 0
        while reach < count // 2:
            if step == len(rounds):
                rounds.append([])
            rounds[step].append((axis, count, position, reach))
            reach = reach * 2
            step = step + 1

    def announce(step):
        for axis, count, position, reach in rounds[step] if step < len(rounds) else ():
            signal(ready.at[position, step], axis, reach)
            signal(ready.at[position, step], axis, count - reach)

    def listen(step):
        for axis, count, position, reach in rounds[step] if step < len(rounds) else ():
            pl.semaphore_wait(ready.at[position, step], 2)

    def send(src, dst, send_sem, recv_sem, axis, target):
        copy = pltpu.make_async_remote_copy(
            src_ref=src, dst_ref=dst, send_sem=send_sem, recv_sem=recv_sem,
            device_id={axis: target}, device_id_type=mesh_id,
        )
        copy.start()

    def arrived(ref, sem):
        pltpu.make_async_copy(ref, ref, sem).wait()

    sub = lax.broadcasted_iota(jnp.int32, (8, width), 0)
    row = lax.rem(sub, 4)
    is0 = row == 0
    is1 = row == 1
    is2 = row == 2
    is3 = row == 3
    low = sub < 4
    sub1 = lax.broadcasted_iota(jnp.int32, (8, LANES), 0)
    row1 = lax.rem(sub1, 4)
    edge1 = (row1 == 0) | (row1 == 3)
    odd1 = lax.rem(sub1, 2) == 1

    def merge(ref):
        return jnp.concatenate([ref[0], ref[1]], axis=0)

    def spread(values, source):
        result = values
        for target in range(4):
            if target > source:
                result = jnp.where(row == target, up(values, target - source), result)
            if target < source:
                result = jnp.where(row == target, down(values, source - target), result)
        return result

    def pack(values, chunk):
        first = values[:, 2 * chunk * LANES : (2 * chunk + 1) * LANES]
        second = values[:, (2 * chunk + 1) * LANES : (2 * chunk + 2) * LANES]
        return jnp.where(edge1, first, up(second, 2))

    def rows_out(values, ref):
        ref[0] = jnp.concatenate([values[0:1], values[4:5]], axis=0)
        ref[1] = jnp.concatenate([values[3:4], values[7:8]], axis=0)

    def rows_in(from_prev, from_next):
        a = from_prev[...]
        b = from_next[...]
        return jnp.concatenate(
            [a[0:1], a[0:1], b[0:1], b[0:1], a[1:2], a[1:2], b[1:2], b[1:2]], axis=0
        )

    def planes_out(values, ref):
        ref[0] = values[0:4]
        ref[1] = values[4:8]

    has_prev = gz > 0
    has_next = gz < m - 1

    def halo_y(src, dst, send_sem, recv_sem):
        send(src.at[0], dst.at[1], send_sem, recv_sem, "gy", peer("gy", n - 1))
        send(src.at[1], dst.at[0], send_sem, recv_sem, "gy", peer("gy", 1))

    def halo_z(src, dst, send_sems, recv_sems):
        @pl.when(has_prev)
        def _():
            send(src.at[0], dst.at[1], send_sems.at[0], recv_sems.at[1], "gz", peer("gz", m - 1))

        @pl.when(has_next)
        def _():
            send(src.at[1], dst.at[0], send_sems.at[1], recv_sems.at[0], "gz", peer("gz", 1))

    def halo_z_wait(dst, recv_sems):
        @pl.when(has_prev)
        def _():
            arrived(dst.at[0], recv_sems.at[0])

        @pl.when(has_next)
        def _():
            arrived(dst.at[1], recv_sems.at[1])

    def halo_z_sent(src, send_sems):
        @pl.when(has_prev)
        def _():
            arrived(src.at[0], send_sems.at[0])

        @pl.when(has_next)
        def _():
            arrived(src.at[1], send_sems.at[1])

    loads[0].wait()
    loads[1].wait()
    classes = merge(cls_v)
    bits = [(classes & (1 << k)) != 0 for k in range(4)]

    def lookup(kind):
        scaled = [tbl[kind, c] * CELL_SCALES[kind] for c in range(16)]
        level = [
            jnp.where(bits[0], scaled[2 * c + 1], scaled[2 * c]) for c in range(8)
        ]
        level = [jnp.where(bits[1], level[2 * c + 1], level[2 * c]) for c in range(4)]
        level = [jnp.where(bits[2], level[2 * c + 1], level[2 * c]) for c in range(2)]
        return jnp.where(bits[3], level[1], level[0])

    cond_y = lookup(2)
    cond_z = lookup(3)
    rows_out(cond_y, y0s.at[0])
    planes_out(cond_z, z0s.at[0])
    loads[2].wait()
    latent = merge(lat_v)
    rows_out(latent, y0s.at[1])
    planes_out(latent, z0s.at[1])

    @pl.when(gz == 0)
    def _():
        for ref in [z0r.at[0], z0r.at[1]] + [zr.at[k] for k in range(ITERS)]:
            ref[0] = jnp.zeros((4, width), jnp.float32)

    @pl.when(gz == m - 1)
    def _():
        for ref in [z0r.at[0], z0r.at[1]] + [zr.at[k] for k in range(ITERS)]:
            ref[1] = jnp.zeros((4, width), jnp.float32)

    pl.semaphore_wait(barrier, 4)

    halo_z(z0s.at[0], z0r.at[0], h_ss.at[0], h_rs.at[0])
    halo_y(y0s.at[0], y0r.at[0], h_ss.at[0, 2], h_rs.at[0, 2])
    announce(0)
    halo_z(z0s.at[1], z0r.at[1], h_ss.at[1], h_rs.at[1])
    halo_y(y0s.at[1], y0r.at[1], h_ss.at[1, 2], h_rs.at[1, 2])

    reaction = lookup(0)
    cond_x = lookup(1)
    column = lax.broadcasted_iota(jnp.int32, (8, width), 1)
    xl = jnp.where(column >= 1, 0.5 * (cond_x + before(cond_x, 1)), 0.0)
    xu = jnp.where(column < width - 1, 0.5 * (cond_x + after(cond_x, 1)), 0.0)
    loads[3].wait()
    loads[4].wait()
    observed = merge(msk_v).astype(jnp.float32)
    counts = merge(cnt_v).astype(jnp.float32)
    growth = jnp.exp(latent)
    intensity = observed * growth

    listen(0)
    announce(1)
    arrived(y0r.at[0], h_rs.at[0, 2])
    halo_z_wait(z0r.at[0], h_rs.at[0])
    listen(1)
    announce(2)
    top = gy == 0
    bottom = gy == n - 1
    edge_y = rows_in(y0r.at[0, 0], y0r.at[0, 1])
    prev_y = jnp.where(is0, edge_y, up(cond_y, 1))
    next_y = jnp.where(is3, edge_y, down(cond_y, 1))
    yl = 0.5 * (cond_y + prev_y)
    yu = 0.5 * (cond_y + next_y)
    yl = jnp.where(is0 & top, 0.0, yl)
    yu = jnp.where(is3 & bottom, 0.0, yu)
    edge_z = merge(z0r.at[0])
    inner = 0.5 * (cond_z + up(cond_z, 4))
    outer = 0.5 * (cond_z + edge_z)
    closed = jnp.where(low, jnp.where(gz == 0, 1, 0), jnp.where(gz == m - 1, 1, 0)) == 1
    outer = jnp.where(closed, 0.0, outer)
    zl = jnp.where(low, outer, inner)
    zu = jnp.where(low, inner, outer)
    half = 0.5 * (reaction + intensity + (zl + zu))
    px = half + xl + xu
    py = half + yl + yu

    def put(name, values):
        coef[COEFS.index(name)] = values

    def get(name):
        return coef[COEFS.index(name)]

    def vput(name, values):
        vec[VECS.index(name)] = values

    def vget(name):
        return vec[VECS.index(name)]

    for name, values in (
        ("px", px), ("py", py), ("xl", xl), ("xu", xu), ("yl", yl), ("yu", yu),
        ("za", inner), ("zb", outer),
    ):
        put(name, values)

    d0 = spread(py, 0)
    d1 = spread(py, 1)
    d2 = spread(py, 2)
    a1 = spread(yl, 1)
    a2 = spread(yl, 2)
    l0 = spread(yl, 0)
    l3 = spread(yl, 3)
    minor0 = d1 * d2 - a2 * a2
    inv_det = 1.0 / (d0 * minor0 - a1 * a1 * d2)
    i00 = minor0 * inv_det
    i01 = a1 * d2 * inv_det
    i02 = a1 * a2 * inv_det
    i11 = d0 * d2 * inv_det
    i12 = a2 * d0 * inv_det
    i22 = (d0 * d1 - a1 * a1) * inv_det
    put("e0", jnp.where(is3, 1.0, l0 * i00))
    put("eu1", jnp.where(is3, l3 * i22, 0.0))
    put("eu2", jnp.where(is3, l3 * i12, 0.0))
    put("eu3", jnp.where(is3, l3 * i02, 0.0))
    put("ed1", jnp.where(is0, l0 * i01, 0.0))
    put("ed2", jnp.where(is0, l0 * i02, 0.0))
    put("g0", jnp.where(is0, i00, jnp.where(is1, i11, jnp.where(is2, i22, 0.0))))
    put("gd1", jnp.where(is0, i01, jnp.where(is1, i12, 0.0)))
    put("gd2", jnp.where(is0, i02, 0.0))
    put("gu1", jnp.where(is1, i01, jnp.where(is2, i12, 0.0)))
    put("gu2", jnp.where(is2, i02, 0.0))
    put("pp", l0 * jnp.where(is0, i00, jnp.where(is1, i01, jnp.where(is2, i02, 0.0))))
    put("qq", jnp.where(is3, 1.0, l3 * jnp.where(is0, i02, jnp.where(is1, i12, i22))))
    main = jnp.where(is3, py - l3 * l3 * i22, -(l0 * l0 * i00))
    link = jnp.where(is3, l3 * i02 * l0, 0.0)
    for chunk in range(n):
        fs[chunk, 0] = pack(main, chunk)
        fs[chunk, 1] = pack(link, chunk)

    def exchange(src, dst, sems):
        dst[gy] = src[gy]
        for offset in far_first(n):
            target = peer("gy", offset)
            send(src.at[target], dst.at[gy], sems.at[0], sems.at[1], "gy", target)

    def received(dst, sems):
        arrived(dst.at[pl.ds(0, n - 1)], sems.at[1])

    listen(2)
    exchange(fs, fr, f_sem)

    arrived(y0r.at[1], h_rs.at[1, 2])
    halo_z_wait(z0r.at[1], h_rs.at[1])
    edge_y = rows_in(y0r.at[1, 0], y0r.at[1, 1])
    edge_z = merge(z0r.at[1])
    center_q = reaction + xl + xu + yl + yu + zl + zu
    applied = (
        center_q * latent - xl * before(latent, 1) - xu * after(latent, 1)
        - yl * jnp.where(is0, edge_y, up(latent, 1))
        - yu * jnp.where(is3, edge_y, down(latent, 1))
        - inner * up(latent, 4) - outer * edge_z
    )
    rhs = observed * (counts - growth) - applied
    vput("r", rhs)

    def forward(k, values):
        gathered = (
            get("e0") * values
            + get("eu1") * up(values, 1) + get("eu2") * up(values, 2) + get("eu3") * up(values, 3)
            + get("ed1") * down(values, 1) + get("ed2") * down(values, 2)
        )
        for chunk in range(n):
            as_[k, chunk] = pack(gathered, chunk)
        exchange(as_.at[k], ar.at[k], a_sem.at[k])

    def x_factors():
        diagonal = get("px")
        band = get("xu")
        stride = 1
        level = 0
        while stride < width:
            inverse = 1.0 / diagonal
            scaled = band * inverse
            ahead = band * after(inverse, stride)
            wb[level] = before(scaled, stride)
            wa[level] = ahead
            diagonal = diagonal - before(scaled * band, stride) - ahead * band
            band = ahead * after(band, stride)
            stride = stride * 2
            level = level + 1
        xinv[...] = 1.0 / diagonal

    def solve_x(values):
        stride = 1
        level = 0
        while stride < width:
            values = values + wb[level] * before(values, stride) + wa[level] * after(values, stride)
            stride = stride * 2
            level = level + 1
        return values * xinv[...]

    def line_factors():
        received(fr, f_sem)
        inverse = None
        for i in range(n):
            diagonal = fr[i, 0]
            if i + 1 < n:
                diagonal = diagonal + up(fr[i + 1, 0], 3)
            diagonal = jnp.where(odd1, diagonal, 1.0)
            if i > 0:
                off = jnp.where(odd1, fr[i, 1], 0.0)
                scale = off * inverse
                smul[i] = scale
                diagonal = diagonal - scale * off
            inverse = 1.0 / diagonal
            sinv[i] = inverse

    def solve_separators(k):
        received(ar.at[k], a_sem.at[k])
        carried = None
        for i in range(n):
            right = ar[k, i]
            if i + 1 < n:
                right = right + up(ar[k, i + 1], 3)
            carried = right if i == 0 else right + smul[i] * carried
            sol[i] = carried
        solved = None
        for i in range(n - 1, -1, -1):
            solved = sol[i] * sinv[i] if i == n - 1 else sol[i] * sinv[i] + smul[i + 1] * solved
            sol[i] = solved
        for i in range(n):
            below = sol[i - 1] if i > 0 else jnp.zeros((8, LANES), jnp.float32)
            bs[k, i] = jnp.where(odd1, sol[i], up(below, 5))
        exchange(bs.at[k], br.at[k], b_sem.at[k])

    def unpack(k):
        parts = []
        for chunk in range(n):
            block = br[k, chunk]
            parts += [block, up(block, 6)]
        return jnp.concatenate(parts, axis=1)

    def apply_pair(k, name, middle, extra=None):
        values = vget(name)
        forward(k, values)
        if k == 0:
            x_factors()
        if extra is not None:
            extra()
        along_x = solve_x(vget(name))
        vput("ax", along_x)
        rows_out(along_x, ys.at[k])
        halo_y(ys.at[k], yr.at[k], k_ss.at[k, 2], k_rs.at[k, 2])
        if k == 0:
            line_factors()
        values = vget(name)
        vput(
            "ay",
            get("g0") * values + get("gu1") * up(values, 1) + get("gu2") * up(values, 2)
            + get("gd1") * down(values, 1) + get("gd2") * down(values, 2),
        )
        solve_separators(k)
        if middle is not None:
            middle()
        arrived(yr.at[k], k_rs.at[k, 2])
        along_x = vget("ax")
        edge = rows_in(yr.at[k, 0], yr.at[k, 1])
        vput(
            "part",
            2.0 * vget(name) + get("py") * along_x
            - get("yl") * jnp.where(is0, edge, up(along_x, 1))
            - get("yu") * jnp.where(is3, edge, down(along_x, 1)),
        )
        received(br.at[k], b_sem.at[k])
        ends = unpack(k)
        along_y = vget("ay") + get("pp") * spread(ends, 0) + get("qq") * spread(ends, 3)
        total = vget("ax") + along_y
        planes_out(total, zs.at[k])
        halo_z(zs.at[k], zr.at[k], k_ss.at[k], k_rs.at[k])
        image = (
            vget("part") + get("px") * along_y
            - get("xl") * before(along_y, 1) - get("xu") * after(along_y, 1)
            - get("za") * up(total, 4)
        )
        halo_z_wait(zr.at[k], k_rs.at[k])
        image = image - get("zb") * merge(zr.at[k])
        return total, image

    def fold(first, second):
        product = first * second
        acc = product[:, 0:LANES]
        for t in range(1, tiles):
            acc = acc + product[:, t * LANES : (t + 1) * LANES]
        return jnp.sum(jnp.sum(acc, axis=0, keepdims=True), axis=1, keepdims=True)

    lane = lax.broadcasted_iota(jnp.int32, (1, LANES), 1)

    def reduce_start(k, sums):
        packed = jnp.zeros((1, LANES), jnp.float32)
        for index, value in enumerate(sums):
            packed = jnp.where(lane == index, value, packed)
        p1s[k] = packed
        p1r[k, gy] = packed
        for offset in far_first(n):
            send(p1s.at[k], p1r.at[k, gy], p1_sem.at[k, 0], p1_sem.at[k, 1], "gy", peer("gy", offset))

    def reduce_middle(k):
        arrived(p1r.at[k, pl.ds(0, n - 1)], p1_sem.at[k, 1])
        total = p1r[k, 0]
        for i in range(1, n):
            total = total + p1r[k, i]
        p2s[k] = total
        p2r[k, gz] = total
        for offset in far_first(m):
            send(p2s.at[k], p2r.at[k, gz], p2_sem.at[k, 0], p2_sem.at[k, 1], "gz", peer("gz", offset))

    def reduce_end(k, count):
        arrived(p2r.at[k, pl.ds(0, m - 1)], p2_sem.at[k, 1])
        total = p2r[k, 0]
        for i in range(1, m):
            total = total + p2r[k, i]
        return [total[:, index : index + 1] for index in range(count)]

    u0, w0 = apply_pair(0, "r", None)
    vput("u0", u0)
    vput("w0", w0)

    def start0():
        reduce_start(0, (fold(vget("r"), vget("u0")), fold(vget("u0"), vget("w0"))))

    def middle0():
        reduce_middle(0)

    q0, z0 = apply_pair(1, "w0", middle0, start0)
    vput("q0", q0)
    vput("z0", z0)
    g0, e0 = reduce_end(0, 2)
    alpha0 = g0 / e0
    r1 = vget("r") - alpha0 * vget("w0")
    u1 = vget("u0") - alpha0 * vget("q0")
    w1 = vget("w0") - alpha0 * vget("z0")
    vput("r", r1)
    vput("u1", u1)
    vput("w1", w1)

    def start1():
        reduce_start(
            1,
            (
                fold(vget("r"), vget("u1")),
                fold(vget("u1"), vget("w1")),
                fold(vget("u1"), vget("w0")),
            ),
        )

    def middle1():
        reduce_middle(1)

    q1, z1 = apply_pair(2, "w1", middle1, start1)
    g1, uw1, c1 = reduce_end(1, 3)
    beta1 = g1 / g0
    e1 = uw1 + 2.0 * beta1 * c1 + beta1 * beta1 * e0
    alpha1 = g1 / e1
    s1 = vget("w1") + beta1 * vget("w0")
    r2 = vget("r") - alpha1 * s1
    u2 = vget("u1") - alpha1 * (q1 + beta1 * vget("q0"))
    w2 = vget("w1") - alpha1 * (z1 + beta1 * vget("z0"))
    reduce_start(2, (fold(r2, u2), fold(u2, w2), fold(u2, s1)))
    reduce_middle(2)
    dir1 = vget("u1") + beta1 * vget("u0")
    done = alpha0 * vget("u0") + alpha1 * dir1
    g2, uw2, c2 = reduce_end(2, 3)
    beta2 = g2 / g1
    e2 = uw2 + 2.0 * beta2 * c2 + beta2 * beta2 * e1
    alpha2 = g2 / e2
    result = done + alpha2 * (u2 + beta2 * dir1)
    out[0] = result[0:4]
    out[1] = result[4:8]
    for index in range(2):
        halo_z_sent(z0s.at[index], h_ss.at[index])
        arrived(y0s.at[index], h_ss.at[index, 2])
    arrived(fs.at[pl.ds(0, n - 1)], f_sem.at[0])
    for k in range(ITERS):
        arrived(as_.at[k, pl.ds(0, n - 1)], a_sem.at[k, 0])
        arrived(bs.at[k, pl.ds(0, n - 1)], b_sem.at[k, 0])
        halo_z_sent(zs.at[k], k_ss.at[k])
        arrived(ys.at[k], k_ss.at[k, 2])
        arrived(p1r.at[k, pl.ds(0, n - 1)], p1_sem.at[k, 0])
        arrived(p2r.at[k, pl.ds(0, m - 1)], p2_sem.at[k, 0])


def shards(latent, event_counts, survey_mask, class_ids, class_table):
    planes, rows, width = latent.shape
    n = lax.axis_size("gy")
    m = lax.axis_size("gz")
    assert planes == 2 and rows == 4 and width == n * 2 * LANES
    levels = 0
    while (1 << levels) < width:
        levels = levels + 1
    f32 = jnp.float32
    dma = pltpu.SemaphoreType.DMA
    vmem = pltpu.VMEM
    block = (2, 4, width)
    scratch = [
        vmem(block, f32), vmem(block, jnp.int32), vmem(block, jnp.int32), vmem(block, jnp.int32),
        pltpu.SMEM(class_table.shape, f32), dma((5,)), pltpu.SemaphoreType.REGULAR((2, 3)),
        vmem((2, 2, 2, width), f32), vmem((2, 2, 2, width), f32),
        vmem((2, 2, 4, width), f32), vmem((2, 2, 4, width), f32), dma((2, 3)), dma((2, 3)),
        vmem((n, 2, 8, LANES), f32), vmem((n, 2, 8, LANES), f32), dma((2,)),
        vmem((3, n, 8, LANES), f32), vmem((3, n, 8, LANES), f32), dma((3, 2)),
        vmem((3, n, 8, LANES), f32), vmem((3, n, 8, LANES), f32), dma((3, 2)),
        vmem((3, 2, 2, width), f32), vmem((3, 2, 2, width), f32),
        vmem((3, 2, 4, width), f32), vmem((3, 2, 4, width), f32), dma((3, 3)), dma((3, 3)),
        vmem((3, 1, LANES), f32), vmem((3, n, 1, LANES), f32), dma((3, 2)),
        vmem((3, 1, LANES), f32), vmem((3, m, 1, LANES), f32), dma((3, 2)),
        vmem((levels, 8, width), f32), vmem((levels, 8, width), f32), vmem((8, width), f32),
        vmem((len(COEFS), 8, width), f32), vmem((len(VECS), 8, width), f32),
        vmem((n, 8, LANES), f32), vmem((n, 8, LANES), f32), vmem((n, 8, LANES), f32),
    ]
    anywhere = pl.BlockSpec(memory_space=pl.ANY)
    return pl.pallas_call(
        functools.partial(kernel, n, m, width),
        out_shape=jax.ShapeDtypeStruct(block, f32),
        in_specs=[anywhere] * 5,
        out_specs=pl.BlockSpec(memory_space=pltpu.VMEM),
        scratch_shapes=scratch,
        compiler_params=pltpu.CompilerParams(collective_id=0, has_side_effects=True),
        name="newton",
    )(latent, event_counts, survey_mask, class_ids, class_table)


def solution(mesh):
    placed = (
        P("gz", "gy", None),
        P("gz", "gy", None),
        P("gz", "gy", None),
        P("gz", "gy", None),
        P(),
    )
    return jax.shard_map(
        shards, mesh=mesh, in_specs=placed, out_specs=P("gz", "gy", None), check_vma=False
    )
```

```python
import functools
import jax
import jax.numpy as jnp
from jax import lax
from jax.experimental import pallas as pl
from jax.experimental.pallas import tpu as pltpu
from jax.sharding import PartitionSpec as P

CELL_SCALES = (0.05, 4.0, 400.0, 1.0)
LANES = 128
ITERS = 3
COEFS = (
    "e0", "eu1", "eu2", "eu3", "ed1", "ed2",
    "g0", "gu1", "gu2", "gd1", "gd2", "pp", "qq",
    "px", "py", "xl", "xu", "yl", "yu", "za", "zb",
)
VECS = ("r", "u0", "w0", "q0", "z0", "u1", "w1", "s1", "ax", "ay", "part")


def up(values, amount):
    return pltpu.roll(values, amount, 0)


def down(values, amount):
    return pltpu.roll(values, 8 - amount, 0)


def before(values, amount):
    return pltpu.roll(values, amount, 1)


def after(values, amount):
    return pltpu.roll(values, values.shape[1] - amount, 1)


def far_first(count):
    order = sorted(range(1, count), key=lambda o: -min(o, count - o))
    return order


def kernel(
    n, m, width,
    lat_h, cnt_h, msk_h, cls_h, tbl_h,
    out,
    lat_v, cnt_v, msk_v, cls_v, tbl, in_sem, ready,
    y0s, y0r, z0s, z0r, h_ss, h_rs,
    fs, fr, f_sem,
    as_, ar, a_sem,
    bs, br, b_sem,
    ys, yr, zs, zr, k_ss, k_rs,
    hbs, hbr, hb_ss, hb_rs,
    cps, cpr, c_ss, c_rs,
    p1s, p1r, p1_sem,
    p2s, p2r, p2_sem,
    wb, wa, xinv, coef, vec, sol, sinv, smul,
):
    gy = lax.axis_index("gy")
    gz = lax.axis_index("gz")
    tiles = width // LANES

    def peer(axis, offset):
        if axis == "gy":
            return lax.rem(gy + offset, n)
        return lax.rem(gz + offset, m)

    mesh_id = pl.DeviceIdType.MESH

    def signal(sem, axis, offset):
        pl.semaphore_signal(sem, inc=1, device_id={axis: peer(axis, offset)}, device_id_type=mesh_id)

    barrier = pltpu.get_barrier_semaphore()
    near = max(1, n // 4)
    greeted = 2
    for offset in range(near, 0, -1):
        signal(barrier, "gy", offset)
        signal(barrier, "gy", n - offset)
        greeted = greeted + 2
    signal(barrier, "gz", 1)
    signal(barrier, "gz", m - 1)

    loads = []
    for index, (src, dst) in enumerate(
        ((cls_h, cls_v), (tbl_h, tbl), (lat_h, lat_v), (msk_h, msk_v), (cnt_h, cnt_v))
    ):
        copy = pltpu.make_async_copy(src, dst, in_sem.at[index])
        copy.start()
        loads.append(copy)

    reaches = [1]
    while reaches[-1] * 2 < m // 2:
        reaches.append(reaches[-1] * 2)

    def announce_group():
        signal(ready.at[0], "gy", near)
        signal(ready.at[0], "gy", n - near)

    def announce(step):
        if step < len(reaches):
            signal(ready.at[step + 1], "gz", reaches[step])
            signal(ready.at[step + 1], "gz", m - reaches[step])

    def listen(step):
        if step < len(reaches):
            pl.semaphore_wait(ready.at[step + 1], 2)

    def send_diagonal(src, dst, send_sem, recv_sem, row_target, plane_target):
        copy = pltpu.make_async_remote_copy(
            src_ref=src, dst_ref=dst, send_sem=send_sem, recv_sem=recv_sem,
            device_id={"gy": row_target, "gz": plane_target}, device_id_type=mesh_id,
        )
        copy.start()

    def send(src, dst, send_sem, recv_sem, axis, target):
        copy = pltpu.make_async_remote_copy(
            src_ref=src, dst_ref=dst, send_sem=send_sem, recv_sem=recv_sem,
            device_id={axis: target}, device_id_type=mesh_id,
        )
        copy.start()

    def arrived(ref, sem):
        pltpu.make_async_copy(ref, ref, sem).wait()

    sub = lax.broadcasted_iota(jnp.int32, (8, width), 0)
    row = lax.rem(sub, 4)
    is0 = row == 0
    is1 = row == 1
    is2 = row == 2
    is3 = row == 3
    low = sub < 4
    sub1 = lax.broadcasted_iota(jnp.int32, (8, LANES), 0)
    row1 = lax.rem(sub1, 4)
    edge1 = (row1 == 0) | (row1 == 3)
    odd1 = lax.rem(sub1, 2) == 1

    def merge(ref):
        return jnp.concatenate([ref[0], ref[1]], axis=0)

    def spread(values, source):
        result = values
        for target in range(4):
            if target > source:
                result = jnp.where(row == target, up(values, target - source), result)
            if target < source:
                result = jnp.where(row == target, down(values, source - target), result)
        return result

    def pack(values, chunk):
        first = values[:, 2 * chunk * LANES : (2 * chunk + 1) * LANES]
        second = values[:, (2 * chunk + 1) * LANES : (2 * chunk + 2) * LANES]
        return jnp.where(edge1, first, up(second, 2))

    def rows_out(values, ref):
        ref[0] = jnp.concatenate([values[0:1], values[4:5]], axis=0)
        ref[1] = jnp.concatenate([values[3:4], values[7:8]], axis=0)

    def rows_in(from_prev, from_next):
        a = from_prev[...]
        b = from_next[...]
        return jnp.concatenate(
            [a[0:1], a[0:1], b[0:1], b[0:1], a[1:2], a[1:2], b[1:2], b[1:2]], axis=0
        )

    def planes_out(values, ref):
        ref[0] = values[0:4]
        ref[1] = values[4:8]

    has_prev = gz > 0
    has_next = gz < m - 1

    def halo_y(src, dst, send_sem, recv_sem):
        send(src.at[0], dst.at[1], send_sem, recv_sem, "gy", peer("gy", n - 1))
        send(src.at[1], dst.at[0], send_sem, recv_sem, "gy", peer("gy", 1))

    def halo_z(src, dst, send_sems, recv_sems):
        @pl.when(has_prev)
        def _():
            send(src.at[0], dst.at[1], send_sems.at[0], recv_sems.at[1], "gz", peer("gz", m - 1))

        @pl.when(has_next)
        def _():
            send(src.at[1], dst.at[0], send_sems.at[1], recv_sems.at[0], "gz", peer("gz", 1))

    def halo_z_wait(dst, recv_sems):
        @pl.when(has_prev)
        def _():
            arrived(dst.at[0], recv_sems.at[0])

        @pl.when(has_next)
        def _():
            arrived(dst.at[1], recv_sems.at[1])

    def halo_z_sent(src, send_sems):
        @pl.when(has_prev)
        def _():
            arrived(src.at[0], send_sems.at[0])

        @pl.when(has_next)
        def _():
            arrived(src.at[1], send_sems.at[1])

    loads[0].wait()
    loads[1].wait()
    classes = merge(cls_v)
    bits = [(classes & (1 << k)) != 0 for k in range(4)]

    def lookup(kind):
        scaled = [tbl[kind, c] * CELL_SCALES[kind] for c in range(16)]
        level = [
            jnp.where(bits[0], scaled[2 * c + 1], scaled[2 * c]) for c in range(8)
        ]
        level = [jnp.where(bits[1], level[2 * c + 1], level[2 * c]) for c in range(4)]
        level = [jnp.where(bits[2], level[2 * c + 1], level[2 * c]) for c in range(2)]
        return jnp.where(bits[3], level[1], level[0])

    cond_y = lookup(2)
    cond_z = lookup(3)
    rows_out(cond_y, y0s.at[0])
    planes_out(cond_z, z0s.at[0])
    loads[2].wait()
    latent = merge(lat_v)
    rows_out(latent, y0s.at[1])
    planes_out(latent, z0s.at[1])

    @pl.when(gz == 0)
    def _():
        for ref in [z0r.at[0], z0r.at[1], cpr.at[0], cpr.at[1]] + [zr.at[k] for k in range(ITERS)]:
            ref[0] = jnp.zeros((4, width), jnp.float32)
        for k in range(ITERS):
            hbr[k, 0] = jnp.zeros((n, 4, LANES), jnp.float32)

    @pl.when(gz == m - 1)
    def _():
        for ref in [z0r.at[0], z0r.at[1], cpr.at[0], cpr.at[1]] + [zr.at[k] for k in range(ITERS)]:
            ref[1] = jnp.zeros((4, width), jnp.float32)
        for k in range(ITERS):
            hbr[k, 1] = jnp.zeros((n, 4, LANES), jnp.float32)

    pl.semaphore_wait(barrier, greeted)
    announce_group()
    announce(0)

    halo_z(z0s.at[0], z0r.at[0], h_ss.at[0], h_rs.at[0])
    halo_y(y0s.at[0], y0r.at[0], h_ss.at[0, 2], h_rs.at[0, 2])
    halo_z(z0s.at[1], z0r.at[1], h_ss.at[1], h_rs.at[1])
    halo_y(y0s.at[1], y0r.at[1], h_ss.at[1, 2], h_rs.at[1, 2])

    reaction = lookup(0)
    cond_x = lookup(1)
    column = lax.broadcasted_iota(jnp.int32, (8, width), 1)
    xl = jnp.where(column >= 1, 0.5 * (cond_x + before(cond_x, 1)), 0.0)
    xu = jnp.where(column < width - 1, 0.5 * (cond_x + after(cond_x, 1)), 0.0)
    loads[3].wait()
    loads[4].wait()
    observed = merge(msk_v).astype(jnp.float32)
    counts = merge(cnt_v).astype(jnp.float32)
    growth = jnp.exp(latent)
    intensity = observed * growth

    arrived(y0r.at[0], h_rs.at[0, 2])
    halo_z_wait(z0r.at[0], h_rs.at[0])
    top = gy == 0
    bottom = gy == n - 1
    edge_y = rows_in(y0r.at[0, 0], y0r.at[0, 1])
    prev_y = jnp.where(is0, edge_y, up(cond_y, 1))
    next_y = jnp.where(is3, edge_y, down(cond_y, 1))
    yl = 0.5 * (cond_y + prev_y)
    yu = 0.5 * (cond_y + next_y)
    yl = jnp.where(is0 & top, 0.0, yl)
    yu = jnp.where(is3 & bottom, 0.0, yu)
    edge_z = merge(z0r.at[0])
    inner = 0.5 * (cond_z + up(cond_z, 4))
    outer = 0.5 * (cond_z + edge_z)
    closed = jnp.where(low, jnp.where(gz == 0, 1, 0), jnp.where(gz == m - 1, 1, 0)) == 1
    outer = jnp.where(closed, 0.0, outer)
    zl = jnp.where(low, outer, inner)
    zu = jnp.where(low, inner, outer)
    half = 0.5 * (reaction + intensity + (zl + zu))
    px = half + xl + xu
    py = half + yl + yu

    def put(name, values):
        coef[COEFS.index(name)] = values

    def get(name):
        return coef[COEFS.index(name)]

    def vput(name, values):
        vec[VECS.index(name)] = values

    def vget(name):
        return vec[VECS.index(name)]

    for name, values in (
        ("px", px), ("py", py), ("xl", xl), ("xu", xu), ("yl", yl), ("yu", yu),
        ("za", inner), ("zb", outer),
    ):
        put(name, values)

    d0 = spread(py, 0)
    d1 = spread(py, 1)
    d2 = spread(py, 2)
    a1 = spread(yl, 1)
    a2 = spread(yl, 2)
    l0 = spread(yl, 0)
    l3 = spread(yl, 3)
    minor0 = d1 * d2 - a2 * a2
    inv_det = 1.0 / (d0 * minor0 - a1 * a1 * d2)
    i00 = minor0 * inv_det
    i01 = a1 * d2 * inv_det
    i02 = a1 * a2 * inv_det
    i11 = d0 * d2 * inv_det
    i12 = a2 * d0 * inv_det
    i22 = (d0 * d1 - a1 * a1) * inv_det
    put("e0", jnp.where(is3, 1.0, l0 * i00))
    put("eu1", jnp.where(is3, l3 * i22, 0.0))
    put("eu2", jnp.where(is3, l3 * i12, 0.0))
    put("eu3", jnp.where(is3, l3 * i02, 0.0))
    put("ed1", jnp.where(is0, l0 * i01, 0.0))
    put("ed2", jnp.where(is0, l0 * i02, 0.0))
    put("g0", jnp.where(is0, i00, jnp.where(is1, i11, jnp.where(is2, i22, 0.0))))
    put("gd1", jnp.where(is0, i01, jnp.where(is1, i12, 0.0)))
    put("gd2", jnp.where(is0, i02, 0.0))
    put("gu1", jnp.where(is1, i01, jnp.where(is2, i12, 0.0)))
    put("gu2", jnp.where(is2, i02, 0.0))
    put("pp", l0 * jnp.where(is0, i00, jnp.where(is1, i01, jnp.where(is2, i02, 0.0))))
    put("qq", jnp.where(is3, 1.0, l3 * jnp.where(is0, i02, jnp.where(is1, i12, i22))))
    main = jnp.where(is3, py - l3 * l3 * i22, -(l0 * l0 * i00))
    link = jnp.where(is3, l3 * i02 * l0, 0.0)
    for chunk in range(n):
        fs[chunk, 0] = pack(main, chunk)
        fs[chunk, 1] = pack(link, chunk)

    def exchange(src, dst, sems):
        dst[gy] = src[gy]
        for offset in far_first(n):
            target = peer("gy", offset)
            send(src.at[target], dst.at[gy], sems.at[0], sems.at[1], "gy", target)

    def received(dst, sems):
        arrived(dst.at[pl.ds(0, n - 1)], sems.at[1])

    pl.semaphore_wait(ready.at[0], 2)
    signal(ready.at[4], "gz", 1)
    signal(ready.at[4], "gz", m - 1)
    listen(0)
    announce(1)
    exchange(fs, fr, f_sem)
    for index, name in enumerate(("pp", "qq")):
        planes_out(get(name), cps.at[index])
        halo_z(cps.at[index], cpr.at[index], c_ss.at[index], c_rs.at[index])

    arrived(y0r.at[1], h_rs.at[1, 2])
    halo_z_wait(z0r.at[1], h_rs.at[1])
    edge_y = rows_in(y0r.at[1, 0], y0r.at[1, 1])
    edge_z = merge(z0r.at[1])
    center_q = reaction + xl + xu + yl + yu + zl + zu
    applied = (
        center_q * latent - xl * before(latent, 1) - xu * after(latent, 1)
        - yl * jnp.where(is0, edge_y, up(latent, 1))
        - yu * jnp.where(is3, edge_y, down(latent, 1))
        - inner * up(latent, 4) - outer * edge_z
    )
    rhs = observed * (counts - growth) - applied
    vput("r", rhs)

    def forward(k, values):
        gathered = (
            get("e0") * values
            + get("eu1") * up(values, 1) + get("eu2") * up(values, 2) + get("eu3") * up(values, 3)
            + get("ed1") * down(values, 1) + get("ed2") * down(values, 2)
        )
        for chunk in range(n):
            as_[k, chunk] = pack(gathered, chunk)
        exchange(as_.at[k], ar.at[k], a_sem.at[k])

    def x_factors():
        diagonal = get("px")
        band = get("xu")
        stride = 1
        level = 0
        while stride < width:
            inverse = 1.0 / diagonal
            scaled = band * inverse
            ahead = band * after(inverse, stride)
            wb[level] = before(scaled, stride)
            wa[level] = ahead
            diagonal = diagonal - before(scaled * band, stride) - ahead * band
            band = ahead * after(band, stride)
            stride = stride * 2
            level = level + 1
        xinv[...] = 1.0 / diagonal

    def solve_x(values):
        stride = 1
        level = 0
        while stride < width:
            values = values + wb[level] * before(values, stride) + wa[level] * after(values, stride)
            stride = stride * 2
            level = level + 1
        return values * xinv[...]

    def line_factors():
        received(fr, f_sem)
        inverse = None
        for i in range(n):
            diagonal = fr[i, 0]
            if i + 1 < n:
                diagonal = diagonal + up(fr[i + 1, 0], 3)
            diagonal = jnp.where(odd1, diagonal, 1.0)
            if i > 0:
                off = jnp.where(odd1, fr[i, 1], 0.0)
                scale = off * inverse
                smul[i] = scale
                diagonal = diagonal - scale * off
            inverse = 1.0 / diagonal
            sinv[i] = inverse

    def solve_separators(k):
        received(ar.at[k], a_sem.at[k])
        carried = None
        for i in range(n):
            right = ar[k, i]
            if i + 1 < n:
                right = right + up(ar[k, i + 1], 3)
            carried = right if i == 0 else right + smul[i] * carried
            sol[i] = carried
        solved = None
        for i in range(n - 1, -1, -1):
            solved = sol[i] * sinv[i] if i == n - 1 else sol[i] * sinv[i] + smul[i + 1] * solved
            sol[i] = solved
        for i in range(n):
            below = sol[i - 1] if i > 0 else jnp.zeros((8, LANES), jnp.float32)
            block = jnp.where(odd1, sol[i], up(below, 5))
            bs[k, i] = block
            hbs[k, 0, i] = squeeze(block)
            hbs[k, 1, i] = squeeze(up(block, 4))
        if k == 0:
            pl.semaphore_wait(ready.at[4], 2)

        @pl.when(has_prev)
        def _():
            for offset in far_first(n) + [0]:
                target = peer("gy", offset)
                send_diagonal(
                    hbs.at[k, 0, target], hbr.at[k, 1, gy], hb_ss.at[k, 0], hb_rs.at[k, 1],
                    target, peer("gz", m - 1),
                )

        @pl.when(has_next)
        def _():
            for offset in far_first(n) + [0]:
                target = peer("gy", offset)
                send_diagonal(
                    hbs.at[k, 1, target], hbr.at[k, 0, gy], hb_ss.at[k, 1], hb_rs.at[k, 0],
                    target, peer("gz", 1),
                )

        exchange(bs.at[k], br.at[k], b_sem.at[k])

    def squeeze(block):
        return jnp.where(sub1 == 0, block, jnp.where(sub1 == 3, down(block, 2), down(block, 1)))[0:4]

    def unpack_halo(k, first):
        parts = []
        for chunk in range(n):
            for part in range(2):
                pair = [
                    jnp.broadcast_to(hbr[k, side, chunk, first + part : first + part + 1], (8, LANES))
                    for side in range(2)
                ]
                parts.append(jnp.where(sub1 < 4, pair[0], pair[1]))
        return jnp.concatenate(parts, axis=1)

    def unpack(k):
        parts = []
        for chunk in range(n):
            block = br[k, chunk]
            parts += [block, up(block, 6)]
        return jnp.concatenate(parts, axis=1)

    def apply_pair(k, name, middle, extra=None):
        values = vget(name)
        forward(k, values)
        if k == 0:
            x_factors()
        if extra is not None:
            extra()
        along_x = solve_x(vget(name))
        vput("ax", along_x)
        rows_out(along_x, ys.at[k])
        halo_y(ys.at[k], yr.at[k], k_ss.at[k, 2], k_rs.at[k, 2])
        if k == 0:
            line_factors()
        values = vget(name)
        inner_y = (
            get("g0") * values + get("gu1") * up(values, 1) + get("gu2") * up(values, 2)
            + get("gd1") * down(values, 1) + get("gd2") * down(values, 2)
        )
        vput("ay", inner_y)
        planes_out(vget("ax") + inner_y, zs.at[k])
        halo_z(zs.at[k], zr.at[k], k_ss.at[k], k_rs.at[k])
        solve_separators(k)
        if k == 0:
            listen(1)
            announce(2)
        if middle is not None:
            middle()
        arrived(yr.at[k], k_rs.at[k, 2])
        along_x = vget("ax")
        edge = rows_in(yr.at[k, 0], yr.at[k, 1])
        halo_z_wait(zr.at[k], k_rs.at[k])
        if k == 0:
            for index in range(2):
                halo_z_wait(cpr.at[index], c_rs.at[index])
        vput(
            "part",
            2.0 * vget(name) + get("py") * along_x
            - get("yl") * jnp.where(is0, edge, up(along_x, 1))
            - get("yu") * jnp.where(is3, edge, down(along_x, 1))
            - get("zb") * merge(zr.at[k]),
        )
        received(br.at[k], b_sem.at[k])
        ends = unpack(k)
        along_y = vget("ay") + get("pp") * spread(ends, 0) + get("qq") * spread(ends, 3)
        total = vget("ax") + along_y
        image = (
            vget("part") + get("px") * along_y
            - get("xl") * before(along_y, 1) - get("xu") * after(along_y, 1)
            - get("za") * up(total, 4)
        )
        halo_z_wait(hbr.at[k], hb_rs.at[k])
        image = image - get("zb") * (
            merge(cpr.at[0]) * unpack_halo(k, 0) + merge(cpr.at[1]) * unpack_halo(k, 2)
        )
        return total, image

    def fold(first, second):
        product = first * second
        acc = product[:, 0:LANES]
        for t in range(1, tiles):
            acc = acc + product[:, t * LANES : (t + 1) * LANES]
        return jnp.sum(jnp.sum(acc, axis=0, keepdims=True), axis=1, keepdims=True)

    lane = lax.broadcasted_iota(jnp.int32, (1, LANES), 1)

    def reduce_start(k, sums):
        packed = jnp.zeros((1, LANES), jnp.float32)
        for index, value in enumerate(sums):
            packed = jnp.where(lane == index, value, packed)
        p1s[k] = packed
        p1r[k, gy] = packed
        for offset in far_first(n):
            send(p1s.at[k], p1r.at[k, gy], p1_sem.at[k, 0], p1_sem.at[k, 1], "gy", peer("gy", offset))

    def reduce_middle(k):
        arrived(p1r.at[k, pl.ds(0, n - 1)], p1_sem.at[k, 1])
        total = p1r[k, 0]
        for i in range(1, n):
            total = total + p1r[k, i]
        p2s[k] = total
        p2r[k, gz] = total
        for offset in far_first(m):
            send(p2s.at[k], p2r.at[k, gz], p2_sem.at[k, 0], p2_sem.at[k, 1], "gz", peer("gz", offset))

    def reduce_end(k, count):
        arrived(p2r.at[k, pl.ds(0, m - 1)], p2_sem.at[k, 1])
        total = p2r[k, 0]
        for i in range(1, m):
            total = total + p2r[k, i]
        return [total[:, index : index + 1] for index in range(count)]

    u0, w0 = apply_pair(0, "r", None)
    vput("u0", u0)
    vput("w0", w0)

    listen(2)

    def start0():
        reduce_start(0, (fold(vget("r"), vget("u0")), fold(vget("u0"), vget("w0"))))

    def middle0():
        reduce_middle(0)

    q0, z0 = apply_pair(1, "w0", middle0, start0)
    vput("q0", q0)
    vput("z0", z0)
    g0, e0 = reduce_end(0, 2)
    alpha0 = g0 / e0
    r1 = vget("r") - alpha0 * vget("w0")
    u1 = vget("u0") - alpha0 * vget("q0")
    w1 = vget("w0") - alpha0 * vget("z0")
    vput("r", r1)
    vput("u1", u1)
    vput("w1", w1)

    def start1():
        reduce_start(
            1,
            (
                fold(vget("r"), vget("u1")),
                fold(vget("u1"), vget("w1")),
                fold(vget("u1"), vget("w0")),
            ),
        )

    def middle1():
        reduce_middle(1)

    q1, z1 = apply_pair(2, "w1", middle1, start1)
    g1, uw1, c1 = reduce_end(1, 3)
    beta1 = g1 / g0
    e1 = uw1 + 2.0 * beta1 * c1 + beta1 * beta1 * e0
    alpha1 = g1 / e1
    s1 = vget("w1") + beta1 * vget("w0")
    r2 = vget("r") - alpha1 * s1
    u2 = vget("u1") - alpha1 * (q1 + beta1 * vget("q0"))
    w2 = vget("w1") - alpha1 * (z1 + beta1 * vget("z0"))
    reduce_start(2, (fold(r2, u2), fold(u2, w2), fold(u2, s1)))
    reduce_middle(2)
    dir1 = vget("u1") + beta1 * vget("u0")
    done = alpha0 * vget("u0") + alpha1 * dir1
    g2, uw2, c2 = reduce_end(2, 3)
    beta2 = g2 / g1
    e2 = uw2 + 2.0 * beta2 * c2 + beta2 * beta2 * e1
    alpha2 = g2 / e2
    result = done + alpha2 * (u2 + beta2 * dir1)
    out[0] = result[0:4]
    out[1] = result[4:8]
    for index in range(2):
        halo_z_sent(z0s.at[index], h_ss.at[index])
        arrived(y0s.at[index], h_ss.at[index, 2])
        halo_z_sent(cps.at[index], c_ss.at[index])
    arrived(fs.at[pl.ds(0, n - 1)], f_sem.at[0])
    for k in range(ITERS):
        arrived(as_.at[k, pl.ds(0, n - 1)], a_sem.at[k, 0])
        arrived(bs.at[k, pl.ds(0, n - 1)], b_sem.at[k, 0])
        halo_z_sent(zs.at[k], k_ss.at[k])
        halo_z_sent(hbs.at[k], hb_ss.at[k])
        arrived(ys.at[k], k_ss.at[k, 2])
        arrived(p1r.at[k, pl.ds(0, n - 1)], p1_sem.at[k, 0])
        arrived(p2r.at[k, pl.ds(0, m - 1)], p2_sem.at[k, 0])


def shards(latent, event_counts, survey_mask, class_ids, class_table):
    planes, rows, width = latent.shape
    n = lax.axis_size("gy")
    m = lax.axis_size("gz")
    assert planes == 2 and rows == 4 and width == n * 2 * LANES
    levels = 0
    while (1 << levels) < width:
        levels = levels + 1
    f32 = jnp.float32
    dma = pltpu.SemaphoreType.DMA
    vmem = pltpu.VMEM
    block = (2, 4, width)
    scratch = [
        vmem(block, f32), vmem(block, jnp.int32), vmem(block, jnp.int32), vmem(block, jnp.int32),
        pltpu.SMEM(class_table.shape, f32), dma((5,)), pltpu.SemaphoreType.REGULAR((5,)),
        vmem((2, 2, 2, width), f32), vmem((2, 2, 2, width), f32),
        vmem((2, 2, 4, width), f32), vmem((2, 2, 4, width), f32), dma((2, 3)), dma((2, 3)),
        vmem((n, 2, 8, LANES), f32), vmem((n, 2, 8, LANES), f32), dma((2,)),
        vmem((3, n, 8, LANES), f32), vmem((3, n, 8, LANES), f32), dma((3, 2)),
        vmem((3, n, 8, LANES), f32), vmem((3, n, 8, LANES), f32), dma((3, 2)),
        vmem((3, 2, 2, width), f32), vmem((3, 2, 2, width), f32),
        vmem((3, 2, 4, width), f32), vmem((3, 2, 4, width), f32), dma((3, 3)), dma((3, 3)),
        vmem((3, 2, n, 4, LANES), f32), vmem((3, 2, n, 4, LANES), f32), dma((3, 2)), dma((3, 2)),
        vmem((2, 2, 4, width), f32), vmem((2, 2, 4, width), f32), dma((2, 2)), dma((2, 2)),
        vmem((3, 1, LANES), f32), vmem((3, n, 1, LANES), f32), dma((3, 2)),
        vmem((3, 1, LANES), f32), vmem((3, m, 1, LANES), f32), dma((3, 2)),
        vmem((levels, 8, width), f32), vmem((levels, 8, width), f32), vmem((8, width), f32),
        vmem((len(COEFS), 8, width), f32), vmem((len(VECS), 8, width), f32),
        vmem((n, 8, LANES), f32), vmem((n, 8, LANES), f32), vmem((n, 8, LANES), f32),
    ]
    anywhere = pl.BlockSpec(memory_space=pl.ANY)
    return pl.pallas_call(
        functools.partial(kernel, n, m, width),
        out_shape=jax.ShapeDtypeStruct(block, f32),
        in_specs=[anywhere] * 5,
        out_specs=pl.BlockSpec(memory_space=pltpu.VMEM),
        scratch_shapes=scratch,
        compiler_params=pltpu.CompilerParams(collective_id=0, has_side_effects=True),
        name="newton",
    )(latent, event_counts, survey_mask, class_ids, class_table)


def solution(mesh):
    placed = (
        P("gz", "gy", None),
        P("gz", "gy", None),
        P("gz", "gy", None),
        P("gz", "gy", None),
        P(),
    )
    return jax.shard_map(
        shards, mesh=mesh, in_specs=placed, out_specs=P("gz", "gy", None), check_vma=False
    )
```

```python
import functools
import jax
import jax.numpy as jnp
from jax import lax
from jax.experimental import pallas as pl
from jax.experimental.pallas import tpu as pltpu
from jax.sharding import PartitionSpec as P

CELL_SCALES = (0.05, 4.0, 400.0, 1.0)
LANES = 128
ITERS = 3
COEFS = (
    "e0", "eu1", "eu2", "eu3", "ed1", "ed2",
    "g0", "gu1", "gu2", "gd1", "gd2", "pp", "qq",
    "px", "py", "xl", "xu", "yl", "yu", "za", "zb", "hp", "hq",
)
VECS = ("r", "u0", "w0", "q0", "z0", "u1", "w1", "s1", "ax", "ay", "part")


def up(values, amount):
    return pltpu.roll(values, amount, 0)


def down(values, amount):
    return pltpu.roll(values, 8 - amount, 0)


def before(values, amount):
    return pltpu.roll(values, amount, 1)


def after(values, amount):
    return pltpu.roll(values, values.shape[1] - amount, 1)


def far_first(count):
    order = sorted(range(1, count), key=lambda o: -min(o, count - o))
    return order


def hops_first(count):
    side = 1
    while side * side < count:
        side = side * 2

    def hops(offset):
        return sum(min(part, side - part) for part in (offset % side, offset // side))

    return sorted(range(1, count), key=lambda offset: -hops(offset))


def kernel(
    n, m, width,
    lat_h, cnt_h, msk_h, cls_h, tbl_h,
    out,
    lat_v, cnt_v, msk_v, cls_v, tbl, in_sem, ready,
    y0s, y0r, z0s, z0r, h_ss, h_rs,
    fs, fr, f_sem,
    as_, ar, a_sem,
    bs, br, b_sem,
    ys, yr, zs, zr, k_ss, k_rs,
    hbs, hbr, hb_ss, hb_rs,
    cps, cpr, c_ss, c_rs,
    p1s, p1r, p1_sem,
    p2s, p2r, p2_sem,
    wb, wa, xinv, coef, vec, sol, sinv, smul,
):
    gy = lax.axis_index("gy")
    gz = lax.axis_index("gz")
    tiles = width // LANES

    def peer(axis, offset):
        if axis == "gy":
            return lax.rem(gy + offset, n)
        return lax.rem(gz + offset, m)

    mesh_id = pl.DeviceIdType.MESH

    def signal(sem, axis, offset):
        pl.semaphore_signal(sem, inc=1, device_id={axis: peer(axis, offset)}, device_id_type=mesh_id)

    barrier = pltpu.get_barrier_semaphore()
    near = max(1, n // 4)
    greeted = 2
    for offset in range(near, 0, -1):
        signal(barrier, "gy", offset)
        signal(barrier, "gy", n - offset)
        greeted = greeted + 2
    signal(barrier, "gz", 1)
    signal(barrier, "gz", m - 1)

    loads = []
    for index, (src, dst) in enumerate(
        ((cls_h, cls_v), (tbl_h, tbl), (lat_h, lat_v), (msk_h, msk_v), (cnt_h, cnt_v))
    ):
        copy = pltpu.make_async_copy(src, dst, in_sem.at[index])
        copy.start()
        loads.append(copy)

    reaches = [1]
    while reaches[-1] * 2 < m // 2:
        reaches.append(reaches[-1] * 2)

    def announce_group():
        signal(ready.at[0], "gy", near)
        signal(ready.at[0], "gy", n - near)

    def announce(step):
        if step < len(reaches):
            signal(ready.at[step + 1], "gz", reaches[step])
            signal(ready.at[step + 1], "gz", m - reaches[step])

    def listen(step):
        if step < len(reaches):
            pl.semaphore_wait(ready.at[step + 1], 2)

    def send_diagonal(src, dst, send_sem, recv_sem, row_target, plane_target):
        copy = pltpu.make_async_remote_copy(
            src_ref=src, dst_ref=dst, send_sem=send_sem, recv_sem=recv_sem,
            device_id={"gy": row_target, "gz": plane_target}, device_id_type=mesh_id,
        )
        copy.start()

    def send(src, dst, send_sem, recv_sem, axis, target):
        copy = pltpu.make_async_remote_copy(
            src_ref=src, dst_ref=dst, send_sem=send_sem, recv_sem=recv_sem,
            device_id={axis: target}, device_id_type=mesh_id,
        )
        copy.start()

    def arrived(ref, sem):
        pltpu.make_async_copy(ref, ref, sem).wait()

    sub = lax.broadcasted_iota(jnp.int32, (8, width), 0)
    row = lax.rem(sub, 4)
    is0 = row == 0
    is1 = row == 1
    is2 = row == 2
    is3 = row == 3
    low = sub < 4
    sub1 = lax.broadcasted_iota(jnp.int32, (8, LANES), 0)
    row1 = lax.rem(sub1, 4)
    edge1 = (row1 == 0) | (row1 == 3)
    odd1 = lax.rem(sub1, 2) == 1

    def merge(ref):
        return jnp.concatenate([ref[0], ref[1]], axis=0)

    def spread(values, source):
        result = values
        for target in range(4):
            if target > source:
                result = jnp.where(row == target, up(values, target - source), result)
            if target < source:
                result = jnp.where(row == target, down(values, source - target), result)
        return result

    def pack(values, chunk):
        first = values[:, 2 * chunk * LANES : (2 * chunk + 1) * LANES]
        second = values[:, (2 * chunk + 1) * LANES : (2 * chunk + 2) * LANES]
        return jnp.where(edge1, first, up(second, 2))

    def rows_out(values, ref):
        ref[0] = jnp.concatenate([values[0:1], values[4:5]], axis=0)
        ref[1] = jnp.concatenate([values[3:4], values[7:8]], axis=0)

    def rows_in(from_prev, from_next):
        a = from_prev[...]
        b = from_next[...]
        return jnp.concatenate(
            [a[0:1], a[0:1], b[0:1], b[0:1], a[1:2], a[1:2], b[1:2], b[1:2]], axis=0
        )

    def planes_out(values, ref):
        ref[0] = values[0:4]
        ref[1] = values[4:8]

    has_prev = gz > 0
    has_next = gz < m - 1

    def halo_y(src, dst, send_sem, recv_sem):
        send(src.at[0], dst.at[1], send_sem, recv_sem, "gy", peer("gy", n - 1))
        send(src.at[1], dst.at[0], send_sem, recv_sem, "gy", peer("gy", 1))

    def halo_z(src, dst, send_sems, recv_sems):
        @pl.when(has_prev)
        def _():
            send(src.at[0], dst.at[1], send_sems.at[0], recv_sems.at[1], "gz", peer("gz", m - 1))

        @pl.when(has_next)
        def _():
            send(src.at[1], dst.at[0], send_sems.at[1], recv_sems.at[0], "gz", peer("gz", 1))

    def halo_z_wait(dst, recv_sems):
        @pl.when(has_prev)
        def _():
            arrived(dst.at[0], recv_sems.at[0])

        @pl.when(has_next)
        def _():
            arrived(dst.at[1], recv_sems.at[1])

    def halo_z_sent(src, send_sems):
        @pl.when(has_prev)
        def _():
            arrived(src.at[0], send_sems.at[0])

        @pl.when(has_next)
        def _():
            arrived(src.at[1], send_sems.at[1])

    loads[0].wait()
    loads[1].wait()
    classes = merge(cls_v)
    bits = [(classes & (1 << k)) != 0 for k in range(4)]

    def lookup(kind):
        scaled = [tbl[kind, c] * CELL_SCALES[kind] for c in range(16)]
        level = [
            jnp.where(bits[0], scaled[2 * c + 1], scaled[2 * c]) for c in range(8)
        ]
        level = [jnp.where(bits[1], level[2 * c + 1], level[2 * c]) for c in range(4)]
        level = [jnp.where(bits[2], level[2 * c + 1], level[2 * c]) for c in range(2)]
        return jnp.where(bits[3], level[1], level[0])

    cond_y = lookup(2)
    cond_z = lookup(3)
    rows_out(cond_y, y0s.at[0])
    planes_out(cond_z, z0s.at[0])
    loads[2].wait()
    latent = merge(lat_v)
    rows_out(latent, y0s.at[1])
    planes_out(latent, z0s.at[1])

    @pl.when(gz == 0)
    def _():
        for ref in [z0r.at[0], z0r.at[1], cpr.at[0], cpr.at[1]] + [zr.at[k] for k in range(ITERS)]:
            ref[0] = jnp.zeros((4, width), jnp.float32)
        for k in range(ITERS):
            hbr[k, 0] = jnp.zeros((n, 4, LANES), jnp.float32)

    @pl.when(gz == m - 1)
    def _():
        for ref in [z0r.at[0], z0r.at[1], cpr.at[0], cpr.at[1]] + [zr.at[k] for k in range(ITERS)]:
            ref[1] = jnp.zeros((4, width), jnp.float32)
        for k in range(ITERS):
            hbr[k, 1] = jnp.zeros((n, 4, LANES), jnp.float32)

    pl.semaphore_wait(barrier, greeted)
    announce_group()
    announce(0)

    halo_z(z0s.at[0], z0r.at[0], h_ss.at[0], h_rs.at[0])
    halo_y(y0s.at[0], y0r.at[0], h_ss.at[0, 2], h_rs.at[0, 2])
    halo_z(z0s.at[1], z0r.at[1], h_ss.at[1], h_rs.at[1])
    halo_y(y0s.at[1], y0r.at[1], h_ss.at[1, 2], h_rs.at[1, 2])

    reaction = lookup(0)
    cond_x = lookup(1)
    column = lax.broadcasted_iota(jnp.int32, (8, width), 1)
    xl = jnp.where(column >= 1, 0.5 * (cond_x + before(cond_x, 1)), 0.0)
    xu = jnp.where(column < width - 1, 0.5 * (cond_x + after(cond_x, 1)), 0.0)
    loads[3].wait()
    loads[4].wait()
    observed = merge(msk_v).astype(jnp.float32)
    counts = merge(cnt_v).astype(jnp.float32)
    growth = jnp.exp(latent)
    intensity = observed * growth

    arrived(y0r.at[0], h_rs.at[0, 2])
    halo_z_wait(z0r.at[0], h_rs.at[0])
    top = gy == 0
    bottom = gy == n - 1
    edge_y = rows_in(y0r.at[0, 0], y0r.at[0, 1])
    prev_y = jnp.where(is0, edge_y, up(cond_y, 1))
    next_y = jnp.where(is3, edge_y, down(cond_y, 1))
    yl = 0.5 * (cond_y + prev_y)
    yu = 0.5 * (cond_y + next_y)
    yl = jnp.where(is0 & top, 0.0, yl)
    yu = jnp.where(is3 & bottom, 0.0, yu)
    edge_z = merge(z0r.at[0])
    inner = 0.5 * (cond_z + up(cond_z, 4))
    outer = 0.5 * (cond_z + edge_z)
    closed = jnp.where(low, jnp.where(gz == 0, 1, 0), jnp.where(gz == m - 1, 1, 0)) == 1
    outer = jnp.where(closed, 0.0, outer)
    zl = jnp.where(low, outer, inner)
    zu = jnp.where(low, inner, outer)
    half = 0.5 * (reaction + intensity + (zl + zu))
    px = half + xl + xu
    py = half + yl + yu

    def put(name, values):
        coef[COEFS.index(name)] = values

    def get(name):
        return coef[COEFS.index(name)]

    def vput(name, values):
        vec[VECS.index(name)] = values

    def vget(name):
        return vec[VECS.index(name)]

    for name, values in (
        ("px", px), ("py", py), ("xl", xl), ("xu", xu), ("yl", yl), ("yu", yu),
        ("za", inner), ("zb", outer),
    ):
        put(name, values)

    d0 = spread(py, 0)
    d1 = spread(py, 1)
    d2 = spread(py, 2)
    a1 = spread(yl, 1)
    a2 = spread(yl, 2)
    l0 = spread(yl, 0)
    l3 = spread(yl, 3)
    minor0 = d1 * d2 - a2 * a2
    inv_det = 1.0 / (d0 * minor0 - a1 * a1 * d2)
    i00 = minor0 * inv_det
    i01 = a1 * d2 * inv_det
    i02 = a1 * a2 * inv_det
    i11 = d0 * d2 * inv_det
    i12 = a2 * d0 * inv_det
    i22 = (d0 * d1 - a1 * a1) * inv_det
    put("e0", jnp.where(is3, 1.0, l0 * i00))
    put("eu1", jnp.where(is3, l3 * i22, 0.0))
    put("eu2", jnp.where(is3, l3 * i12, 0.0))
    put("eu3", jnp.where(is3, l3 * i02, 0.0))
    put("ed1", jnp.where(is0, l0 * i01, 0.0))
    put("ed2", jnp.where(is0, l0 * i02, 0.0))
    put("g0", jnp.where(is0, i00, jnp.where(is1, i11, jnp.where(is2, i22, 0.0))))
    put("gd1", jnp.where(is0, i01, jnp.where(is1, i12, 0.0)))
    put("gd2", jnp.where(is0, i02, 0.0))
    put("gu1", jnp.where(is1, i01, jnp.where(is2, i12, 0.0)))
    put("gu2", jnp.where(is2, i02, 0.0))
    put("pp", l0 * jnp.where(is0, i00, jnp.where(is1, i01, jnp.where(is2, i02, 0.0))))
    put("qq", jnp.where(is3, 1.0, l3 * jnp.where(is0, i02, jnp.where(is1, i12, i22))))
    main = jnp.where(is3, py - l3 * l3 * i22, -(l0 * l0 * i00))
    link = jnp.where(is3, l3 * i02 * l0, 0.0)
    for chunk in range(n):
        block = pack(link, chunk)
        fs[chunk, 0:8] = pack(main, chunk)
        fs[chunk, 8:12] = jnp.where(
            sub1 == 0, down(block, 3), jnp.where(sub1 == 1, down(block, 4), jnp.where(sub1 == 2, down(block, 5), up(block, 2)))
        )[0:4]

    def exchange(src, dst, sems):
        dst[gy] = src[gy]
        for offset in far_first(n):
            target = peer("gy", offset)
            send(src.at[target], dst.at[gy], sems.at[0], sems.at[1], "gy", target)

    def received(dst, sems):
        arrived(dst.at[pl.ds(0, n - 1)], sems.at[1])

    pl.semaphore_wait(ready.at[0], 2)
    signal(ready.at[4], "gz", 1)
    signal(ready.at[4], "gz", m - 1)
    listen(0)
    announce(1)
    exchange(fs, fr, f_sem)
    for index, name in enumerate(("pp", "qq")):
        planes_out(get(name), cps.at[index])
        halo_z(cps.at[index], cpr.at[index], c_ss.at[index], c_rs.at[index])

    arrived(y0r.at[1], h_rs.at[1, 2])
    halo_z_wait(z0r.at[1], h_rs.at[1])
    edge_y = rows_in(y0r.at[1, 0], y0r.at[1, 1])
    edge_z = merge(z0r.at[1])
    center_q = reaction + xl + xu + yl + yu + zl + zu
    applied = (
        center_q * latent - xl * before(latent, 1) - xu * after(latent, 1)
        - yl * jnp.where(is0, edge_y, up(latent, 1))
        - yu * jnp.where(is3, edge_y, down(latent, 1))
        - inner * up(latent, 4) - outer * edge_z
    )
    rhs = observed * (counts - growth) - applied
    vput("r", rhs)

    def forward(k, values):
        gathered = (
            get("e0") * values
            + get("eu1") * up(values, 1) + get("eu2") * up(values, 2) + get("eu3") * up(values, 3)
            + get("ed1") * down(values, 1) + get("ed2") * down(values, 2)
        )
        for chunk in range(n):
            as_[k, chunk] = pack(gathered, chunk)
        exchange(as_.at[k], ar.at[k], a_sem.at[k])

    def x_factors():
        diagonal = get("px")
        band = get("xu")
        stride = 1
        level = 0
        while stride < width:
            inverse = 1.0 / diagonal
            scaled = band * inverse
            ahead = band * after(inverse, stride)
            wb[level] = before(scaled, stride)
            wa[level] = ahead
            diagonal = diagonal - before(scaled * band, stride) - ahead * band
            band = ahead * after(band, stride)
            stride = stride * 2
            level = level + 1
        xinv[...] = 1.0 / diagonal

    def solve_x(values):
        stride = 1
        level = 0
        while stride < width:
            values = values + wb[level] * before(values, stride) + wa[level] * after(values, stride)
            stride = stride * 2
            level = level + 1
        return values * xinv[...]

    def line_factors():
        received(fr, f_sem)
        inverse = None
        for i in range(n):
            diagonal = fr[i, 0:8]
            if i + 1 < n:
                diagonal = diagonal + up(fr[i + 1, 0:8], 3)
            diagonal = jnp.where(odd1, diagonal, 1.0)
            if i > 0:
                rows = fr[i, 8:12]
                rows = jnp.concatenate([rows, rows], axis=0)
                off = jnp.where(
                    sub1 == 3, up(rows, 3),
                    jnp.where(sub1 == 5, rows, jnp.where(sub1 == 7, up(rows, 1), up(rows, 2))),
                )
                off = jnp.where(odd1, off, 0.0)
                scale = off * inverse
                smul[i] = scale
                diagonal = diagonal - scale * off
            inverse = 1.0 / diagonal
            sinv[i] = inverse

    def solve_separators(k):
        received(ar.at[k], a_sem.at[k])
        carried = None
        for i in range(n):
            right = ar[k, i]
            if i + 1 < n:
                right = right + up(ar[k, i + 1], 3)
            carried = right if i == 0 else right + smul[i] * carried
            sol[i] = carried
        solved = None
        for i in range(n - 1, -1, -1):
            solved = sol[i] * sinv[i] if i == n - 1 else sol[i] * sinv[i] + smul[i + 1] * solved
            sol[i] = solved
        for i in range(n):
            below = sol[i - 1] if i > 0 else jnp.zeros((8, LANES), jnp.float32)
            block = jnp.where(odd1, sol[i], up(below, 5))
            bs[k, i] = block
            hbs[k, 0, i] = squeeze(block)
            hbs[k, 1, i] = squeeze(up(block, 4))
        if k == 0:
            pl.semaphore_wait(ready.at[4], 2)

        @pl.when(has_prev)
        def _():
            for offset in far_first(n) + [0]:
                target = peer("gy", offset)
                send_diagonal(
                    hbs.at[k, 0, target], hbr.at[k, 1, gy], hb_ss.at[k, 0], hb_rs.at[k, 1],
                    target, peer("gz", m - 1),
                )

        @pl.when(has_next)
        def _():
            for offset in far_first(n) + [0]:
                target = peer("gy", offset)
                send_diagonal(
                    hbs.at[k, 1, target], hbr.at[k, 0, gy], hb_ss.at[k, 1], hb_rs.at[k, 0],
                    target, peer("gz", 1),
                )

        exchange(bs.at[k], br.at[k], b_sem.at[k])

    def squeeze(block):
        return jnp.where(sub1 == 0, block, jnp.where(sub1 == 3, down(block, 2), down(block, 1)))[0:4]

    def unpack_halo(k, first):
        parts = []
        for chunk in range(n):
            for part in range(2):
                pair = [
                    jnp.broadcast_to(hbr[k, side, chunk, first + part : first + part + 1], (8, LANES))
                    for side in range(2)
                ]
                parts.append(jnp.where(sub1 < 4, pair[0], pair[1]))
        return jnp.concatenate(parts, axis=1)

    def unpack(k):
        parts = []
        for chunk in range(n):
            block = br[k, chunk]
            parts += [block, up(block, 6)]
        return jnp.concatenate(parts, axis=1)

    def apply_pair(k, name, middle, extra=None):
        values = vget(name)
        forward(k, values)
        if k == 0:
            x_factors()
        if extra is not None:
            extra()
        along_x = solve_x(vget(name))
        vput("ax", along_x)
        rows_out(along_x, ys.at[k])
        halo_y(ys.at[k], yr.at[k], k_ss.at[k, 2], k_rs.at[k, 2])
        if k == 0:
            line_factors()
        values = vget(name)
        inner_y = (
            get("g0") * values + get("gu1") * up(values, 1) + get("gu2") * up(values, 2)
            + get("gd1") * down(values, 1) + get("gd2") * down(values, 2)
        )
        vput("ay", inner_y)
        planes_out(vget("ax") + inner_y, zs.at[k])
        halo_z(zs.at[k], zr.at[k], k_ss.at[k], k_rs.at[k])
        solve_separators(k)
        if k == 0:
            listen(1)
            announce(2)
        if middle is not None:
            middle()
        arrived(yr.at[k], k_rs.at[k, 2])
        along_x = vget("ax")
        edge = rows_in(yr.at[k, 0], yr.at[k, 1])
        halo_z_wait(zr.at[k], k_rs.at[k])
        if k == 0:
            for index in range(2):
                halo_z_wait(cpr.at[index], c_rs.at[index])
            put("hp", get("zb") * merge(cpr.at[0]))
            put("hq", get("zb") * merge(cpr.at[1]))
        vput(
            "part",
            2.0 * vget(name) + get("py") * along_x
            - get("yl") * jnp.where(is0, edge, up(along_x, 1))
            - get("yu") * jnp.where(is3, edge, down(along_x, 1))
            - get("zb") * merge(zr.at[k]),
        )
        received(br.at[k], b_sem.at[k])
        ends = unpack(k)
        along_y = vget("ay") + get("pp") * spread(ends, 0) + get("qq") * spread(ends, 3)
        total = vget("ax") + along_y
        image = (
            vget("part") + get("px") * along_y
            - get("xl") * before(along_y, 1) - get("xu") * after(along_y, 1)
            - get("za") * up(total, 4)
        )
        halo_z_wait(hbr.at[k], hb_rs.at[k])
        image = image - get("hp") * unpack_halo(k, 0) - get("hq") * unpack_halo(k, 2)
        return total, image

    def fold(first, second):
        product = first * second
        acc = product[:, 0:LANES]
        for t in range(1, tiles):
            acc = acc + product[:, t * LANES : (t + 1) * LANES]
        return jnp.sum(jnp.sum(acc, axis=0, keepdims=True), axis=1, keepdims=True)

    lane = lax.broadcasted_iota(jnp.int32, (1, LANES), 1)

    def reduce_start(k, sums):
        packed = jnp.zeros((1, LANES), jnp.float32)
        for index, value in enumerate(sums):
            packed = jnp.where(lane == index, value, packed)
        p1s[k] = packed
        p1r[k, gy] = packed
        for offset in far_first(n):
            send(p1s.at[k], p1r.at[k, gy], p1_sem.at[k, 0], p1_sem.at[k, 1], "gy", peer("gy", offset))

    def reduce_middle(k):
        arrived(p1r.at[k, pl.ds(0, n - 1)], p1_sem.at[k, 1])
        total = p1r[k, 0]
        for i in range(1, n):
            total = total + p1r[k, i]
        p2s[k] = total
        p2r[k, gz] = total
        for offset in hops_first(m):
            send(p2s.at[k], p2r.at[k, gz], p2_sem.at[k, 0], p2_sem.at[k, 1], "gz", peer("gz", offset))

    def reduce_end(k, count):
        arrived(p2r.at[k, pl.ds(0, m - 1)], p2_sem.at[k, 1])
        total = p2r[k, 0]
        for i in range(1, m):
            total = total + p2r[k, i]
        return [total[:, index : index + 1] for index in range(count)]

    u0, w0 = apply_pair(0, "r", None)
    vput("u0", u0)
    vput("w0", w0)

    listen(2)

    def start0():
        reduce_start(0, (fold(vget("r"), vget("u0")), fold(vget("u0"), vget("w0"))))

    def middle0():
        reduce_middle(0)

    q0, z0 = apply_pair(1, "w0", middle0, start0)
    vput("q0", q0)
    vput("z0", z0)
    g0, e0 = reduce_end(0, 2)
    alpha0 = g0 / e0
    r1 = vget("r") - alpha0 * vget("w0")
    u1 = vget("u0") - alpha0 * vget("q0")
    w1 = vget("w0") - alpha0 * vget("z0")
    vput("r", r1)
    vput("u1", u1)
    vput("w1", w1)

    def start1():
        reduce_start(
            1,
            (
                fold(vget("r"), vget("u1")),
                fold(vget("u1"), vget("w1")),
                fold(vget("u1"), vget("w0")),
            ),
        )

    def middle1():
        reduce_middle(1)

    q1, z1 = apply_pair(2, "w1", middle1, start1)
    g1, uw1, c1 = reduce_end(1, 3)
    beta1 = g1 / g0
    e1 = uw1 + 2.0 * beta1 * c1 + beta1 * beta1 * e0
    alpha1 = g1 / e1
    s1 = vget("w1") + beta1 * vget("w0")
    r2 = vget("r") - alpha1 * s1
    u2 = vget("u1") - alpha1 * (q1 + beta1 * vget("q0"))
    w2 = vget("w1") - alpha1 * (z1 + beta1 * vget("z0"))
    reduce_start(2, (fold(r2, u2), fold(u2, w2), fold(u2, s1)))
    reduce_middle(2)
    dir1 = vget("u1") + beta1 * vget("u0")
    done = alpha0 * vget("u0") + alpha1 * dir1
    g2, uw2, c2 = reduce_end(2, 3)
    beta2 = g2 / g1
    e2 = uw2 + 2.0 * beta2 * c2 + beta2 * beta2 * e1
    alpha2 = g2 / e2
    result = done + alpha2 * (u2 + beta2 * dir1)
    out[0] = result[0:4]
    out[1] = result[4:8]
    for index in range(2):
        halo_z_sent(z0s.at[index], h_ss.at[index])
        arrived(y0s.at[index], h_ss.at[index, 2])
        halo_z_sent(cps.at[index], c_ss.at[index])
    arrived(fs.at[pl.ds(0, n - 1)], f_sem.at[0])
    for k in range(ITERS):
        arrived(as_.at[k, pl.ds(0, n - 1)], a_sem.at[k, 0])
        arrived(bs.at[k, pl.ds(0, n - 1)], b_sem.at[k, 0])
        halo_z_sent(zs.at[k], k_ss.at[k])
        halo_z_sent(hbs.at[k], hb_ss.at[k])
        arrived(ys.at[k], k_ss.at[k, 2])
        arrived(p1r.at[k, pl.ds(0, n - 1)], p1_sem.at[k, 0])
        arrived(p2r.at[k, pl.ds(0, m - 1)], p2_sem.at[k, 0])


def shards(latent, event_counts, survey_mask, class_ids, class_table):
    planes, rows, width = latent.shape
    n = lax.axis_size("gy")
    m = lax.axis_size("gz")
    assert planes == 2 and rows == 4 and width == n * 2 * LANES
    levels = 0
    while (1 << levels) < width:
        levels = levels + 1
    f32 = jnp.float32
    dma = pltpu.SemaphoreType.DMA
    vmem = pltpu.VMEM
    block = (2, 4, width)
    scratch = [
        vmem(block, f32), vmem(block, jnp.int32), vmem(block, jnp.int32), vmem(block, jnp.int32),
        pltpu.SMEM(class_table.shape, f32), dma((5,)), pltpu.SemaphoreType.REGULAR((5,)),
        vmem((2, 2, 2, width), f32), vmem((2, 2, 2, width), f32),
        vmem((2, 2, 4, width), f32), vmem((2, 2, 4, width), f32), dma((2, 3)), dma((2, 3)),
        vmem((n, 12, LANES), f32), vmem((n, 12, LANES), f32), dma((2,)),
        vmem((3, n, 8, LANES), f32), vmem((3, n, 8, LANES), f32), dma((3, 2)),
        vmem((3, n, 8, LANES), f32), vmem((3, n, 8, LANES), f32), dma((3, 2)),
        vmem((3, 2, 2, width), f32), vmem((3, 2, 2, width), f32),
        vmem((3, 2, 4, width), f32), vmem((3, 2, 4, width), f32), dma((3, 3)), dma((3, 3)),
        vmem((3, 2, n, 4, LANES), f32), vmem((3, 2, n, 4, LANES), f32), dma((3, 2)), dma((3, 2)),
        vmem((2, 2, 4, width), f32), vmem((2, 2, 4, width), f32), dma((2, 2)), dma((2, 2)),
        vmem((3, 1, LANES), f32), vmem((3, n, 1, LANES), f32), dma((3, 2)),
        vmem((3, 1, LANES), f32), vmem((3, m, 1, LANES), f32), dma((3, 2)),
        vmem((levels, 8, width), f32), vmem((levels, 8, width), f32), vmem((8, width), f32),
        vmem((len(COEFS), 8, width), f32), vmem((len(VECS), 8, width), f32),
        vmem((n, 8, LANES), f32), vmem((n, 8, LANES), f32), vmem((n, 8, LANES), f32),
    ]
    anywhere = pl.BlockSpec(memory_space=pl.ANY)
    return pl.pallas_call(
        functools.partial(kernel, n, m, width),
        out_shape=pltpu.VMEM(block, f32),
        in_specs=[anywhere] * 5,
        out_specs=pl.BlockSpec(memory_space=pltpu.VMEM),
        scratch_shapes=scratch,
        compiler_params=pltpu.CompilerParams(collective_id=0, has_side_effects=True),
        name="newton",
    )(latent, event_counts, survey_mask, class_ids, class_table)


def solution(mesh):
    placed = (
        P("gz", "gy", None),
        P("gz", "gy", None),
        P("gz", "gy", None),
        P("gz", "gy", None),
        P(),
    )
    return jax.shard_map(
        shards, mesh=mesh, in_specs=placed, out_specs=P("gz", "gy", None), check_vma=False
    )
```

```python
import functools
import jax
import jax.numpy as jnp
from jax import lax
from jax.experimental import pallas as pl
from jax.experimental.pallas import tpu as pltpu
from jax.sharding import PartitionSpec as P

CELL_SCALES = (0.05, 4.0, 400.0, 1.0)
LANES = 128
ITERS = 3
COEFS = (
    "e0", "eu1", "eu2", "eu3", "ed1", "ed2",
    "g0", "gu1", "gu2", "gd1", "gd2", "pp", "qq",
    "px", "py", "xl", "xu", "yl", "yu", "za", "zb", "hp", "hq",
)
VECS = ("r", "u0", "w0", "q0", "z0", "u1", "w1", "s1", "ax", "ay", "part")


def up(values, amount):
    return pltpu.roll(values, amount, 0)


def down(values, amount):
    return pltpu.roll(values, 8 - amount, 0)


def before(values, amount):
    return pltpu.roll(values, amount, 1)


def after(values, amount):
    return pltpu.roll(values, values.shape[1] - amount, 1)


def far_first(count):
    order = sorted(range(1, count), key=lambda o: -min(o, count - o))
    return order


def hops_first(count):
    side = 1
    while side * side < count:
        side = side * 2

    def hops(offset):
        return sum(min(part, side - part) for part in (offset % side, offset // side))

    return sorted(range(1, count), key=lambda offset: -hops(offset))


def kernel(
    n, m, width,
    lat_h, cnt_h, msk_h, cls_h, tbl_h,
    out,
    lat_v, cnt_v, msk_v, cls_v, tbl, in_sem, ready,
    y0s, y0r, z0s, z0r, h_ss, h_rs,
    fs, fr, f_sem,
    as_, ar, a_sem,
    bs, br, b_sem,
    ys, yr, zs, zr, k_ss, k_rs,
    hbs, hbr, hb_ss, hb_rs,
    hsr, hs_ss, hs_rs, kps, kpr, kp_sem,
    cps, cpr, c_ss, c_rs,
    p1s, p1r, p1_sem,
    p2s, p2r, p2_sem,
    wb, wa, xinv, coef, vec, sol, sinv, smul, corr,
):
    gy = lax.axis_index("gy")
    gz = lax.axis_index("gz")
    tiles = width // LANES

    def peer(axis, offset):
        if axis == "gy":
            return lax.rem(gy + offset, n)
        return lax.rem(gz + offset, m)

    mesh_id = pl.DeviceIdType.MESH

    def signal(sem, axis, offset):
        pl.semaphore_signal(sem, inc=1, device_id={axis: peer(axis, offset)}, device_id_type=mesh_id)

    barrier = pltpu.get_barrier_semaphore()
    near = max(1, n // 4)
    greeted = 2
    for offset in range(near, 0, -1):
        signal(barrier, "gy", offset)
        signal(barrier, "gy", n - offset)
        greeted = greeted + 2
    signal(barrier, "gz", 1)
    signal(barrier, "gz", m - 1)

    loads = []
    for index, (src, dst) in enumerate(
        ((cls_h, cls_v), (tbl_h, tbl), (lat_h, lat_v), (msk_h, msk_v), (cnt_h, cnt_v))
    ):
        copy = pltpu.make_async_copy(src, dst, in_sem.at[index])
        copy.start()
        loads.append(copy)

    reaches = [1]
    while reaches[-1] * 2 < m // 2:
        reaches.append(reaches[-1] * 2)

    def announce_group():
        signal(ready.at[0], "gy", near)
        signal(ready.at[0], "gy", n - near)

    def announce(step):
        if step < len(reaches):
            signal(ready.at[step + 1], "gz", reaches[step])
            signal(ready.at[step + 1], "gz", m - reaches[step])

    def listen(step):
        if step < len(reaches):
            pl.semaphore_wait(ready.at[step + 1], 2)

    def send_diagonal(src, dst, send_sem, recv_sem, row_target, plane_target):
        copy = pltpu.make_async_remote_copy(
            src_ref=src, dst_ref=dst, send_sem=send_sem, recv_sem=recv_sem,
            device_id={"gy": row_target, "gz": plane_target}, device_id_type=mesh_id,
        )
        copy.start()

    def send(src, dst, send_sem, recv_sem, axis, target):
        copy = pltpu.make_async_remote_copy(
            src_ref=src, dst_ref=dst, send_sem=send_sem, recv_sem=recv_sem,
            device_id={axis: target}, device_id_type=mesh_id,
        )
        copy.start()

    def arrived(ref, sem):
        pltpu.make_async_copy(ref, ref, sem).wait()

    sub = lax.broadcasted_iota(jnp.int32, (8, width), 0)
    row = lax.rem(sub, 4)
    is0 = row == 0
    is1 = row == 1
    is2 = row == 2
    is3 = row == 3
    low = sub < 4
    sub1 = lax.broadcasted_iota(jnp.int32, (8, LANES), 0)
    row1 = lax.rem(sub1, 4)
    edge1 = (row1 == 0) | (row1 == 3)
    odd1 = lax.rem(sub1, 2) == 1

    def merge(ref):
        return jnp.concatenate([ref[0], ref[1]], axis=0)

    def spread(values, source):
        result = values
        for target in range(4):
            if target > source:
                result = jnp.where(row == target, up(values, target - source), result)
            if target < source:
                result = jnp.where(row == target, down(values, source - target), result)
        return result

    def pack(values, chunk):
        first = values[:, 2 * chunk * LANES : (2 * chunk + 1) * LANES]
        second = values[:, (2 * chunk + 1) * LANES : (2 * chunk + 2) * LANES]
        return jnp.where(edge1, first, up(second, 2))

    def rows_out(values, ref):
        ref[0] = jnp.concatenate([values[0:1], values[4:5]], axis=0)
        ref[1] = jnp.concatenate([values[3:4], values[7:8]], axis=0)

    def rows_in(from_prev, from_next):
        a = from_prev[...]
        b = from_next[...]
        return jnp.concatenate(
            [a[0:1], a[0:1], b[0:1], b[0:1], a[1:2], a[1:2], b[1:2], b[1:2]], axis=0
        )

    def planes_out(values, ref):
        ref[0] = values[0:4]
        ref[1] = values[4:8]

    has_prev = gz > 0
    has_next = gz < m - 1

    def halo_y(src, dst, send_sem, recv_sem):
        send(src.at[0], dst.at[1], send_sem, recv_sem, "gy", peer("gy", n - 1))
        send(src.at[1], dst.at[0], send_sem, recv_sem, "gy", peer("gy", 1))

    def halo_z(src, dst, send_sems, recv_sems):
        @pl.when(has_prev)
        def _():
            send(src.at[0], dst.at[1], send_sems.at[0], recv_sems.at[1], "gz", peer("gz", m - 1))

        @pl.when(has_next)
        def _():
            send(src.at[1], dst.at[0], send_sems.at[1], recv_sems.at[0], "gz", peer("gz", 1))

    def halo_z_wait(dst, recv_sems):
        @pl.when(has_prev)
        def _():
            arrived(dst.at[0], recv_sems.at[0])

        @pl.when(has_next)
        def _():
            arrived(dst.at[1], recv_sems.at[1])

    def halo_z_sent(src, send_sems):
        @pl.when(has_prev)
        def _():
            arrived(src.at[0], send_sems.at[0])

        @pl.when(has_next)
        def _():
            arrived(src.at[1], send_sems.at[1])

    loads[0].wait()
    loads[1].wait()
    classes = merge(cls_v)
    bits = [(classes & (1 << k)) != 0 for k in range(4)]

    def lookup(kind):
        scaled = [tbl[kind, c] * CELL_SCALES[kind] for c in range(16)]
        level = [
            jnp.where(bits[0], scaled[2 * c + 1], scaled[2 * c]) for c in range(8)
        ]
        level = [jnp.where(bits[1], level[2 * c + 1], level[2 * c]) for c in range(4)]
        level = [jnp.where(bits[2], level[2 * c + 1], level[2 * c]) for c in range(2)]
        return jnp.where(bits[3], level[1], level[0])

    cond_y = lookup(2)
    cond_z = lookup(3)
    rows_out(cond_y, y0s.at[0])
    planes_out(cond_z, z0s.at[0])
    loads[2].wait()
    latent = merge(lat_v)
    rows_out(latent, y0s.at[1])
    planes_out(latent, z0s.at[1])

    @pl.when(gz == 0)
    def _():
        for ref in [z0r.at[0], z0r.at[1], cpr.at[0], cpr.at[1]] + [zr.at[k] for k in range(ITERS)]:
            ref[0] = jnp.zeros((4, width), jnp.float32)
        for k in range(ITERS):
            hbr[k, 0] = jnp.zeros((n, 4, LANES), jnp.float32)
        for k in range(ITERS - 1):
            hsr[k, 0] = jnp.zeros((n, 4, LANES), jnp.float32)

    @pl.when(gz == m - 1)
    def _():
        for ref in [z0r.at[0], z0r.at[1], cpr.at[0], cpr.at[1]] + [zr.at[k] for k in range(ITERS)]:
            ref[1] = jnp.zeros((4, width), jnp.float32)
        for k in range(ITERS):
            hbr[k, 1] = jnp.zeros((n, 4, LANES), jnp.float32)
        for k in range(ITERS - 1):
            hsr[k, 1] = jnp.zeros((n, 4, LANES), jnp.float32)

    pl.semaphore_wait(barrier, greeted)
    announce_group()
    announce(0)

    halo_z(z0s.at[0], z0r.at[0], h_ss.at[0], h_rs.at[0])
    halo_y(y0s.at[0], y0r.at[0], h_ss.at[0, 2], h_rs.at[0, 2])
    halo_z(z0s.at[1], z0r.at[1], h_ss.at[1], h_rs.at[1])
    halo_y(y0s.at[1], y0r.at[1], h_ss.at[1, 2], h_rs.at[1, 2])

    reaction = lookup(0)
    cond_x = lookup(1)
    column = lax.broadcasted_iota(jnp.int32, (8, width), 1)
    xl = jnp.where(column >= 1, 0.5 * (cond_x + before(cond_x, 1)), 0.0)
    xu = jnp.where(column < width - 1, 0.5 * (cond_x + after(cond_x, 1)), 0.0)
    loads[3].wait()
    loads[4].wait()
    observed = merge(msk_v).astype(jnp.float32)
    counts = merge(cnt_v).astype(jnp.float32)
    growth = jnp.exp(latent)
    intensity = observed * growth

    arrived(y0r.at[0], h_rs.at[0, 2])
    halo_z_wait(z0r.at[0], h_rs.at[0])
    top = gy == 0
    bottom = gy == n - 1
    edge_y = rows_in(y0r.at[0, 0], y0r.at[0, 1])
    prev_y = jnp.where(is0, edge_y, up(cond_y, 1))
    next_y = jnp.where(is3, edge_y, down(cond_y, 1))
    yl = 0.5 * (cond_y + prev_y)
    yu = 0.5 * (cond_y + next_y)
    yl = jnp.where(is0 & top, 0.0, yl)
    yu = jnp.where(is3 & bottom, 0.0, yu)
    edge_z = merge(z0r.at[0])
    inner = 0.5 * (cond_z + up(cond_z, 4))
    outer = 0.5 * (cond_z + edge_z)
    closed = jnp.where(low, jnp.where(gz == 0, 1, 0), jnp.where(gz == m - 1, 1, 0)) == 1
    outer = jnp.where(closed, 0.0, outer)
    zl = jnp.where(low, outer, inner)
    zu = jnp.where(low, inner, outer)
    half = 0.5 * (reaction + intensity + (zl + zu))
    px = half + xl + xu
    py = half + yl + yu

    def put(name, values):
        coef[COEFS.index(name)] = values

    def get(name):
        return coef[COEFS.index(name)]

    def vput(name, values):
        vec[VECS.index(name)] = values

    def vget(name):
        return vec[VECS.index(name)]

    for name, values in (
        ("px", px), ("py", py), ("xl", xl), ("xu", xu), ("yl", yl), ("yu", yu),
        ("za", inner), ("zb", outer),
    ):
        put(name, values)

    d0 = spread(py, 0)
    d1 = spread(py, 1)
    d2 = spread(py, 2)
    a1 = spread(yl, 1)
    a2 = spread(yl, 2)
    l0 = spread(yl, 0)
    l3 = spread(yl, 3)
    minor0 = d1 * d2 - a2 * a2
    inv_det = 1.0 / (d0 * minor0 - a1 * a1 * d2)
    i00 = minor0 * inv_det
    i01 = a1 * d2 * inv_det
    i02 = a1 * a2 * inv_det
    i11 = d0 * d2 * inv_det
    i12 = a2 * d0 * inv_det
    i22 = (d0 * d1 - a1 * a1) * inv_det
    put("e0", jnp.where(is3, 1.0, l0 * i00))
    put("eu1", jnp.where(is3, l3 * i22, 0.0))
    put("eu2", jnp.where(is3, l3 * i12, 0.0))
    put("eu3", jnp.where(is3, l3 * i02, 0.0))
    put("ed1", jnp.where(is0, l0 * i01, 0.0))
    put("ed2", jnp.where(is0, l0 * i02, 0.0))
    put("g0", jnp.where(is0, i00, jnp.where(is1, i11, jnp.where(is2, i22, 0.0))))
    put("gd1", jnp.where(is0, i01, jnp.where(is1, i12, 0.0)))
    put("gd2", jnp.where(is0, i02, 0.0))
    put("gu1", jnp.where(is1, i01, jnp.where(is2, i12, 0.0)))
    put("gu2", jnp.where(is2, i02, 0.0))
    put("pp", l0 * jnp.where(is0, i00, jnp.where(is1, i01, jnp.where(is2, i02, 0.0))))
    put("qq", jnp.where(is3, 1.0, l3 * jnp.where(is0, i02, jnp.where(is1, i12, i22))))
    main = jnp.where(is3, py - l3 * l3 * i22, -(l0 * l0 * i00))
    link = jnp.where(is3, l3 * i02 * l0, 0.0)
    for chunk in range(n):
        block = pack(link, chunk)
        fs[chunk, 0:8] = pack(main, chunk)
        fs[chunk, 8:12] = jnp.where(
            sub1 == 0, down(block, 3), jnp.where(sub1 == 1, down(block, 4), jnp.where(sub1 == 2, down(block, 5), up(block, 2)))
        )[0:4]

    def exchange(src, dst, sems):
        dst[gy] = src[gy]
        for offset in far_first(n):
            target = peer("gy", offset)
            send(src.at[target], dst.at[gy], sems.at[0], sems.at[1], "gy", target)

    def received(dst, sems):
        arrived(dst.at[pl.ds(0, n - 1)], sems.at[1])

    pl.semaphore_wait(ready.at[0], 2)
    signal(ready.at[4], "gz", 1)
    signal(ready.at[4], "gz", m - 1)
    listen(0)
    announce(1)
    exchange(fs, fr, f_sem)
    for index, name in enumerate(("pp", "qq")):
        planes_out(get(name), cps.at[index])
        halo_z(cps.at[index], cpr.at[index], c_ss.at[index], c_rs.at[index])

    arrived(y0r.at[1], h_rs.at[1, 2])
    halo_z_wait(z0r.at[1], h_rs.at[1])
    edge_y = rows_in(y0r.at[1, 0], y0r.at[1, 1])
    edge_z = merge(z0r.at[1])
    center_q = reaction + xl + xu + yl + yu + zl + zu
    applied = (
        center_q * latent - xl * before(latent, 1) - xu * after(latent, 1)
        - yl * jnp.where(is0, edge_y, up(latent, 1))
        - yu * jnp.where(is3, edge_y, down(latent, 1))
        - inner * up(latent, 4) - outer * edge_z
    )
    rhs = observed * (counts - growth) - applied
    vput("r", rhs)

    def gather(values):
        return (
            get("e0") * values
            + get("eu1") * up(values, 1) + get("eu2") * up(values, 2) + get("eu3") * up(values, 3)
            + get("ed1") * down(values, 1) + get("ed2") * down(values, 2)
        )

    def forward(k, values):
        gathered = gather(values)
        for chunk in range(n):
            as_[k, chunk] = pack(gathered, chunk)
        exchange(as_.at[k], ar.at[k], a_sem.at[k])

    def x_factors():
        diagonal = get("px")
        band = get("xu")
        stride = 1
        level = 0
        while stride < width:
            inverse = 1.0 / diagonal
            scaled = band * inverse
            ahead = band * after(inverse, stride)
            wb[level] = before(scaled, stride)
            wa[level] = ahead
            diagonal = diagonal - before(scaled * band, stride) - ahead * band
            band = ahead * after(band, stride)
            stride = stride * 2
            level = level + 1
        xinv[...] = 1.0 / diagonal

    def solve_x(values):
        stride = 1
        level = 0
        while stride < width:
            values = values + wb[level] * before(values, stride) + wa[level] * after(values, stride)
            stride = stride * 2
            level = level + 1
        return values * xinv[...]

    def line_factors():
        received(fr, f_sem)
        inverse = None
        for i in range(n):
            diagonal = fr[i, 0:8]
            if i + 1 < n:
                diagonal = diagonal + up(fr[i + 1, 0:8], 3)
            diagonal = jnp.where(odd1, diagonal, 1.0)
            if i > 0:
                rows = fr[i, 8:12]
                rows = jnp.concatenate([rows, rows], axis=0)
                off = jnp.where(
                    sub1 == 3, up(rows, 3),
                    jnp.where(sub1 == 5, rows, jnp.where(sub1 == 7, up(rows, 1), up(rows, 2))),
                )
                off = jnp.where(odd1, off, 0.0)
                scale = off * inverse
                smul[i] = scale
                diagonal = diagonal - scale * off
            inverse = 1.0 / diagonal
            sinv[i] = inverse

    def correct(k, scale):
        halo_z_wait(hsr.at[k - 1], hs_rs.at[k - 1])
        if k == 1:
            received(kpr, kp_sem)
        for i in range(n):
            shares = []
            for first in (0, 2):
                quarter = [
                    jnp.broadcast_to(hsr[k - 1, side, i, first + part : first + part + 1], (8, LANES))
                    for side in range(2)
                    for part in range(2)
                ]
                shares.append(
                    jnp.where(
                        (sub1 == 0) | (sub1 == 3), quarter[0],
                        jnp.where(
                            (sub1 == 2) | (sub1 == 5), quarter[1],
                            jnp.where((sub1 == 4) | (sub1 == 7), quarter[2], quarter[3]),
                        ),
                    )
                )
            share = kpr[i, 0:8] * shares[0] + kpr[i, 8:16] * shares[1]
            corr[i] = -share if scale is None else scale * share

    def arrived_side(k, i):
        return ar[k, i] if k == 0 else ar[k, i] + corr[i]

    def solve_separators(k):
        received(ar.at[k], a_sem.at[k])
        carried = None
        for i in range(n):
            right = arrived_side(k, i)
            if i + 1 < n:
                right = right + up(arrived_side(k, i + 1), 3)
            carried = right if i == 0 else right + smul[i] * carried
            sol[i] = carried
        solved = None
        for i in range(n - 1, -1, -1):
            solved = sol[i] * sinv[i] if i == n - 1 else sol[i] * sinv[i] + smul[i + 1] * solved
            sol[i] = solved
        for i in range(n):
            below = sol[i - 1] if i > 0 else jnp.zeros((8, LANES), jnp.float32)
            block = jnp.where(odd1, sol[i], up(below, 5))
            bs[k, i] = block
            hbs[k, 0, i] = squeeze(block)
            hbs[k, 1, i] = squeeze(up(block, 4))
        if k == 0:
            pl.semaphore_wait(ready.at[4], 2)

        if k + 1 < ITERS:
            exchange(bs.at[k], br.at[k], b_sem.at[k])
            halo_z(hbs.at[k], hsr.at[k], hs_ss.at[k], hs_rs.at[k])

        @pl.when(has_prev)
        def _():
            for offset in far_first(n) + [0]:
                target = peer("gy", offset)
                send_diagonal(
                    hbs.at[k, 0, target], hbr.at[k, 1, gy], hb_ss.at[k, 0], hb_rs.at[k, 1],
                    target, peer("gz", m - 1),
                )

        @pl.when(has_next)
        def _():
            for offset in far_first(n) + [0]:
                target = peer("gy", offset)
                send_diagonal(
                    hbs.at[k, 1, target], hbr.at[k, 0, gy], hb_ss.at[k, 1], hb_rs.at[k, 0],
                    target, peer("gz", 1),
                )

        if k + 1 == ITERS:
            exchange(bs.at[k], br.at[k], b_sem.at[k])

    def squeeze(block):
        return jnp.where(sub1 == 0, block, jnp.where(sub1 == 3, down(block, 2), down(block, 1)))[0:4]

    def unpack_halo(k, first):
        parts = []
        for chunk in range(n):
            for part in range(2):
                pair = [
                    jnp.broadcast_to(hbr[k, side, chunk, first + part : first + part + 1], (8, LANES))
                    for side in range(2)
                ]
                parts.append(jnp.where(sub1 < 4, pair[0], pair[1]))
        return jnp.concatenate(parts, axis=1)

    def unpack(k):
        parts = []
        for chunk in range(n):
            block = br[k, chunk]
            parts += [block, up(block, 6)]
        return jnp.concatenate(parts, axis=1)

    def apply_pair(k, name, middle, extra=None, scale=None):
        values = vget(name)
        forward(k, values)
        if k == 0:
            x_factors()
        if extra is not None:
            extra()
        along_x = solve_x(vget(name))
        vput("ax", along_x)
        rows_out(along_x, ys.at[k])
        halo_y(ys.at[k], yr.at[k], k_ss.at[k, 2], k_rs.at[k, 2])
        if k == 0:
            line_factors()
        values = vget(name)
        inner_y = (
            get("g0") * values + get("gu1") * up(values, 1) + get("gu2") * up(values, 2)
            + get("gd1") * down(values, 1) + get("gd2") * down(values, 2)
        )
        vput("ay", inner_y)
        planes_out(vget("ax") + inner_y, zs.at[k])
        halo_z(zs.at[k], zr.at[k], k_ss.at[k], k_rs.at[k])
        if k > 0:
            correct(k, scale)
        solve_separators(k)
        if k == 0:
            listen(1)
            announce(2)
            for index in range(2):
                halo_z_wait(cpr.at[index], c_rs.at[index])
                put(("hp", "hq")[index], get("zb") * merge(cpr.at[index]))
            for index, name_h in enumerate(("hp", "hq")):
                gathered = gather(get(name_h))
                for chunk in range(n):
                    kps[chunk, 8 * index : 8 * index + 8] = pack(gathered, chunk)
            exchange(kps, kpr, kp_sem)
        if middle is not None:
            middle()
        arrived(yr.at[k], k_rs.at[k, 2])
        along_x = vget("ax")
        edge = rows_in(yr.at[k, 0], yr.at[k, 1])
        halo_z_wait(zr.at[k], k_rs.at[k])
        vput(
            "part",
            2.0 * vget(name) + get("py") * along_x
            - get("yl") * jnp.where(is0, edge, up(along_x, 1))
            - get("yu") * jnp.where(is3, edge, down(along_x, 1))
            - get("zb") * merge(zr.at[k]),
        )
        received(br.at[k], b_sem.at[k])
        ends = unpack(k)
        along_y = vget("ay") + get("pp") * spread(ends, 0) + get("qq") * spread(ends, 3)
        total = vget("ax") + along_y
        image = (
            vget("part") + get("px") * along_y
            - get("xl") * before(along_y, 1) - get("xu") * after(along_y, 1)
            - get("za") * up(total, 4)
        )
        return total, image

    def halo_share(k):
        halo_z_wait(hbr.at[k], hb_rs.at[k])
        return get("hp") * unpack_halo(k, 0) + get("hq") * unpack_halo(k, 2)

    def fold(first, second):
        product = first * second
        acc = product[:, 0:LANES]
        for t in range(1, tiles):
            acc = acc + product[:, t * LANES : (t + 1) * LANES]
        return jnp.sum(jnp.sum(acc, axis=0, keepdims=True), axis=1, keepdims=True)

    lane = lax.broadcasted_iota(jnp.int32, (1, LANES), 1)

    def reduce_start(k, sums):
        packed = jnp.zeros((1, LANES), jnp.float32)
        for index, value in enumerate(sums):
            packed = jnp.where(lane == index, value, packed)
        p1s[k] = packed
        p1r[k, gy] = packed
        for offset in far_first(n):
            send(p1s.at[k], p1r.at[k, gy], p1_sem.at[k, 0], p1_sem.at[k, 1], "gy", peer("gy", offset))

    def reduce_middle(k):
        arrived(p1r.at[k, pl.ds(0, n - 1)], p1_sem.at[k, 1])
        total = p1r[k, 0]
        for i in range(1, n):
            total = total + p1r[k, i]
        p2s[k] = total
        p2r[k, gz] = total
        for offset in hops_first(m):
            send(p2s.at[k], p2r.at[k, gz], p2_sem.at[k, 0], p2_sem.at[k, 1], "gz", peer("gz", offset))

    def reduce_end(k, count):
        arrived(p2r.at[k, pl.ds(0, m - 1)], p2_sem.at[k, 1])
        total = p2r[k, 0]
        for i in range(1, m):
            total = total + p2r[k, i]
        return [total[:, index : index + 1] for index in range(count)]

    u0, w0 = apply_pair(0, "r", None)
    vput("u0", u0)
    vput("w0", w0)

    listen(2)

    def start0():
        vput("w0", vget("w0") - halo_share(0))
        reduce_start(0, (fold(vget("r"), vget("u0")), fold(vget("u0"), vget("w0"))))

    def middle0():
        reduce_middle(0)

    q0, z0 = apply_pair(1, "w0", middle0, start0)
    vput("q0", q0)
    vput("z0", z0)
    g0, e0 = reduce_end(0, 2)
    alpha0 = g0 / e0
    r1 = vget("r") - alpha0 * vget("w0")
    u1 = vget("u0") - alpha0 * vget("q0")
    w1 = vget("w0") - alpha0 * vget("z0")
    vput("r", r1)
    vput("u1", u1)
    vput("w1", w1)

    def start1():
        share = halo_share(1)
        vput("z0", vget("z0") - share)
        vput("w1", vget("w1") + alpha0 * share)
        reduce_start(
            1,
            (
                fold(vget("r"), vget("u1")),
                fold(vget("u1"), vget("w1")),
                fold(vget("u1"), vget("w0")),
            ),
        )

    def middle1():
        reduce_middle(1)

    q1, z1 = apply_pair(2, "w1", middle1, start1, alpha0)
    z1 = z1 - halo_share(2)
    g1, uw1, c1 = reduce_end(1, 3)
    beta1 = g1 / g0
    e1 = uw1 + 2.0 * beta1 * c1 + beta1 * beta1 * e0
    alpha1 = g1 / e1
    s1 = vget("w1") + beta1 * vget("w0")
    r2 = vget("r") - alpha1 * s1
    u2 = vget("u1") - alpha1 * (q1 + beta1 * vget("q0"))
    w2 = vget("w1") - alpha1 * (z1 + beta1 * vget("z0"))
    reduce_start(2, (fold(r2, u2), fold(u2, w2), fold(u2, s1)))
    reduce_middle(2)
    dir1 = vget("u1") + beta1 * vget("u0")
    done = alpha0 * vget("u0") + alpha1 * dir1
    g2, uw2, c2 = reduce_end(2, 3)
    beta2 = g2 / g1
    e2 = uw2 + 2.0 * beta2 * c2 + beta2 * beta2 * e1
    alpha2 = g2 / e2
    result = done + alpha2 * (u2 + beta2 * dir1)
    out[0] = result[0:4]
    out[1] = result[4:8]
    for index in range(2):
        halo_z_sent(z0s.at[index], h_ss.at[index])
        arrived(y0s.at[index], h_ss.at[index, 2])
        halo_z_sent(cps.at[index], c_ss.at[index])
    for k in range(ITERS - 1):
        halo_z_sent(hbs.at[k], hs_ss.at[k])
    arrived(kps.at[pl.ds(0, n - 1)], kp_sem.at[0])
    arrived(fs.at[pl.ds(0, n - 1)], f_sem.at[0])
    for k in range(ITERS):
        arrived(as_.at[k, pl.ds(0, n - 1)], a_sem.at[k, 0])
        arrived(bs.at[k, pl.ds(0, n - 1)], b_sem.at[k, 0])
        halo_z_sent(zs.at[k], k_ss.at[k])
        halo_z_sent(hbs.at[k], hb_ss.at[k])
        arrived(ys.at[k], k_ss.at[k, 2])
        arrived(p1r.at[k, pl.ds(0, n - 1)], p1_sem.at[k, 0])
        arrived(p2r.at[k, pl.ds(0, m - 1)], p2_sem.at[k, 0])


def shards(latent, event_counts, survey_mask, class_ids, class_table):
    planes, rows, width = latent.shape
    n = lax.axis_size("gy")
    m = lax.axis_size("gz")
    assert planes == 2 and rows == 4 and width == n * 2 * LANES
    levels = 0
    while (1 << levels) < width:
        levels = levels + 1
    f32 = jnp.float32
    dma = pltpu.SemaphoreType.DMA
    vmem = pltpu.VMEM
    block = (2, 4, width)
    scratch = [
        vmem(block, f32), vmem(block, jnp.int32), vmem(block, jnp.int32), vmem(block, jnp.int32),
        pltpu.SMEM(class_table.shape, f32), dma((5,)), pltpu.SemaphoreType.REGULAR((5,)),
        vmem((2, 2, 2, width), f32), vmem((2, 2, 2, width), f32),
        vmem((2, 2, 4, width), f32), vmem((2, 2, 4, width), f32), dma((2, 3)), dma((2, 3)),
        vmem((n, 12, LANES), f32), vmem((n, 12, LANES), f32), dma((2,)),
        vmem((3, n, 8, LANES), f32), vmem((3, n, 8, LANES), f32), dma((3, 2)),
        vmem((3, n, 8, LANES), f32), vmem((3, n, 8, LANES), f32), dma((3, 2)),
        vmem((3, 2, 2, width), f32), vmem((3, 2, 2, width), f32),
        vmem((3, 2, 4, width), f32), vmem((3, 2, 4, width), f32), dma((3, 3)), dma((3, 3)),
        vmem((3, 2, n, 4, LANES), f32), vmem((3, 2, n, 4, LANES), f32), dma((3, 2)), dma((3, 2)),
        vmem((2, 2, n, 4, LANES), f32), dma((2, 2)), dma((2, 2)),
        vmem((n, 16, LANES), f32), vmem((n, 16, LANES), f32), dma((2,)),
        vmem((2, 2, 4, width), f32), vmem((2, 2, 4, width), f32), dma((2, 2)), dma((2, 2)),
        vmem((3, 1, LANES), f32), vmem((3, n, 1, LANES), f32), dma((3, 2)),
        vmem((3, 1, LANES), f32), vmem((3, m, 1, LANES), f32), dma((3, 2)),
        vmem((levels, 8, width), f32), vmem((levels, 8, width), f32), vmem((8, width), f32),
        vmem((len(COEFS), 8, width), f32), vmem((len(VECS), 8, width), f32),
        vmem((n, 8, LANES), f32), vmem((n, 8, LANES), f32), vmem((n, 8, LANES), f32),
        vmem((n, 8, LANES), f32),
    ]
    anywhere = pl.BlockSpec(memory_space=pl.ANY)
    return pl.pallas_call(
        functools.partial(kernel, n, m, width),
        out_shape=pltpu.VMEM(block, f32),
        in_specs=[anywhere] * 5,
        out_specs=pl.BlockSpec(memory_space=pltpu.VMEM),
        scratch_shapes=scratch,
        compiler_params=pltpu.CompilerParams(collective_id=0, has_side_effects=True),
        name="newton",
    )(latent, event_counts, survey_mask, class_ids, class_table)


def solution(mesh):
    placed = (
        P("gz", "gy", None),
        P("gz", "gy", None),
        P("gz", "gy", None),
        P("gz", "gy", None),
        P(),
    )
    return jax.shard_map(
        shards, mesh=mesh, in_specs=placed, out_specs=P("gz", "gy", None), check_vma=False
    )
```

```python
import functools
import jax
import jax.numpy as jnp
from jax import lax
from jax.experimental import pallas as pl
from jax.experimental.pallas import tpu as pltpu
from jax.sharding import PartitionSpec as P

CELL_SCALES = (0.05, 4.0, 400.0, 1.0)
LANES = 128
ITERS = 3
COEFS = (
    "e0", "eu1", "eu2", "eu3", "ed1", "ed2",
    "g0", "gu1", "gu2", "gd1", "gd2", "pp", "qq",
    "px", "py", "xl", "xu", "yl", "yu", "za", "zb", "hp", "hq",
)
VECS = ("r", "u0", "w0", "q0", "z0", "u1", "w1", "s1", "ax", "ay", "part")


def up(values, amount):
    return pltpu.roll(values, amount, 0)


def down(values, amount):
    return pltpu.roll(values, 8 - amount, 0)


def before(values, amount):
    return pltpu.roll(values, amount, 1)


def after(values, amount):
    return pltpu.roll(values, values.shape[1] - amount, 1)


def far_first(count):
    order = sorted(range(1, count), key=lambda o: -min(o, count - o))
    return order


def hops_first(count):
    side = 1
    while side * side < count:
        side = side * 2

    def hops(offset):
        return sum(min(part, side - part) for part in (offset % side, offset // side))

    return sorted(range(1, count), key=lambda offset: -hops(offset))


def kernel(
    n, m, width,
    lat_h, cnt_h, msk_h, cls_h, tbl_h,
    out,
    lat_v, cnt_v, msk_v, cls_v, tbl, in_sem, ready,
    y0s, y0r, z0s, z0r, h_ss, h_rs,
    fs, fr, f_sem,
    as_, ar, a_sem,
    bs, br, b_sem,
    ys, yr, zs, zr, k_ss, k_rs,
    hbs, hbr, hb_ss, hb_rs,
    hsr, hs_ss, hs_rs, kps, kpr, kp_sem,
    cps, cpr, c_ss, c_rs,
    p1s, p1r, p1_sem,
    p2s, p2r, p2_sem,
    wb, wa, xinv, coef, vec, sol, sinv, smul, corr,
):
    gy = lax.axis_index("gy")
    gz = lax.axis_index("gz")
    tiles = width // LANES

    def peer(axis, offset):
        if axis == "gy":
            return lax.rem(gy + offset, n)
        return lax.rem(gz + offset, m)

    mesh_id = pl.DeviceIdType.MESH

    def signal(sem, axis, offset):
        pl.semaphore_signal(sem, inc=1, device_id={axis: peer(axis, offset)}, device_id_type=mesh_id)

    barrier = pltpu.get_barrier_semaphore()
    near = max(1, n // 4)
    greeted = 2
    for offset in range(near, 0, -1):
        signal(barrier, "gy", offset)
        signal(barrier, "gy", n - offset)
        greeted = greeted + 2
    signal(barrier, "gz", 1)
    signal(barrier, "gz", m - 1)

    loads = []
    for index, (src, dst) in enumerate(
        ((cls_h, cls_v), (tbl_h, tbl), (lat_h, lat_v), (msk_h, msk_v), (cnt_h, cnt_v))
    ):
        copy = pltpu.make_async_copy(src, dst, in_sem.at[index])
        copy.start()
        loads.append(copy)

    reaches = [1]
    while reaches[-1] * 2 < m // 2:
        reaches.append(reaches[-1] * 2)

    def announce_group():
        signal(ready.at[0], "gy", near)
        signal(ready.at[0], "gy", n - near)

    def announce(step):
        if step < len(reaches):
            signal(ready.at[step + 1], "gz", reaches[step])
            signal(ready.at[step + 1], "gz", m - reaches[step])

    def listen(step):
        if step < len(reaches):
            pl.semaphore_wait(ready.at[step + 1], 2)

    def send_diagonal(src, dst, send_sem, recv_sem, row_target, plane_target):
        copy = pltpu.make_async_remote_copy(
            src_ref=src, dst_ref=dst, send_sem=send_sem, recv_sem=recv_sem,
            device_id={"gy": row_target, "gz": plane_target}, device_id_type=mesh_id,
        )
        copy.start()

    def send(src, dst, send_sem, recv_sem, axis, target):
        copy = pltpu.make_async_remote_copy(
            src_ref=src, dst_ref=dst, send_sem=send_sem, recv_sem=recv_sem,
            device_id={axis: target}, device_id_type=mesh_id,
        )
        copy.start()

    def arrived(ref, sem):
        pltpu.make_async_copy(ref, ref, sem).wait()

    sub = lax.broadcasted_iota(jnp.int32, (8, width), 0)
    row = lax.rem(sub, 4)
    is0 = row == 0
    is1 = row == 1
    is2 = row == 2
    is3 = row == 3
    low = sub < 4
    sub1 = lax.broadcasted_iota(jnp.int32, (8, LANES), 0)
    row1 = lax.rem(sub1, 4)
    edge1 = (row1 == 0) | (row1 == 3)
    odd1 = lax.rem(sub1, 2) == 1

    def merge(ref):
        return jnp.concatenate([ref[0], ref[1]], axis=0)

    def spread(values, source):
        result = values
        for target in range(4):
            if target > source:
                result = jnp.where(row == target, up(values, target - source), result)
            if target < source:
                result = jnp.where(row == target, down(values, source - target), result)
        return result

    def pack(values, chunk):
        first = values[:, 2 * chunk * LANES : (2 * chunk + 1) * LANES]
        second = values[:, (2 * chunk + 1) * LANES : (2 * chunk + 2) * LANES]
        return jnp.where(edge1, first, up(second, 2))

    def rows_out(values, ref):
        ref[0] = jnp.concatenate([values[0:1], values[4:5]], axis=0)
        ref[1] = jnp.concatenate([values[3:4], values[7:8]], axis=0)

    def rows_in(from_prev, from_next):
        a = from_prev[...]
        b = from_next[...]
        return jnp.concatenate(
            [a[0:1], a[0:1], b[0:1], b[0:1], a[1:2], a[1:2], b[1:2], b[1:2]], axis=0
        )

    def planes_out(values, ref):
        ref[0] = values[0:4]
        ref[1] = values[4:8]

    has_prev = gz > 0
    has_next = gz < m - 1

    def halo_y(src, dst, send_sem, recv_sem):
        send(src.at[0], dst.at[1], send_sem, recv_sem, "gy", peer("gy", n - 1))
        send(src.at[1], dst.at[0], send_sem, recv_sem, "gy", peer("gy", 1))

    def halo_z(src, dst, send_sems, recv_sems):
        @pl.when(has_prev)
        def _():
            send(src.at[0], dst.at[1], send_sems.at[0], recv_sems.at[1], "gz", peer("gz", m - 1))

        @pl.when(has_next)
        def _():
            send(src.at[1], dst.at[0], send_sems.at[1], recv_sems.at[0], "gz", peer("gz", 1))

    def halo_z_wait(dst, recv_sems):
        @pl.when(has_prev)
        def _():
            arrived(dst.at[0], recv_sems.at[0])

        @pl.when(has_next)
        def _():
            arrived(dst.at[1], recv_sems.at[1])

    def halo_z_sent(src, send_sems):
        @pl.when(has_prev)
        def _():
            arrived(src.at[0], send_sems.at[0])

        @pl.when(has_next)
        def _():
            arrived(src.at[1], send_sems.at[1])

    loads[0].wait()
    loads[1].wait()
    classes = merge(cls_v)
    bits = [(classes & (1 << k)) != 0 for k in range(4)]

    def lookup(kind):
        scaled = [tbl[kind, c] * CELL_SCALES[kind] for c in range(16)]
        level = [
            jnp.where(bits[0], scaled[2 * c + 1], scaled[2 * c]) for c in range(8)
        ]
        level = [jnp.where(bits[1], level[2 * c + 1], level[2 * c]) for c in range(4)]
        level = [jnp.where(bits[2], level[2 * c + 1], level[2 * c]) for c in range(2)]
        return jnp.where(bits[3], level[1], level[0])

    cond_y = lookup(2)
    cond_z = lookup(3)
    rows_out(cond_y, y0s.at[0])
    planes_out(cond_z, z0s.at[0])
    loads[2].wait()
    latent = merge(lat_v)
    rows_out(latent, y0s.at[1])
    planes_out(latent, z0s.at[1])

    @pl.when(gz == 0)
    def _():
        for ref in [z0r.at[0], z0r.at[1], cpr.at[0], cpr.at[1]] + [zr.at[k] for k in range(ITERS)]:
            ref[0] = jnp.zeros((4, width), jnp.float32)
        for k in range(ITERS):
            hbr[k, 0] = jnp.zeros((n, 4, LANES), jnp.float32)
        for k in range(ITERS - 1):
            hsr[k, 0] = jnp.zeros((n, 4, LANES), jnp.float32)

    @pl.when(gz == m - 1)
    def _():
        for ref in [z0r.at[0], z0r.at[1], cpr.at[0], cpr.at[1]] + [zr.at[k] for k in range(ITERS)]:
            ref[1] = jnp.zeros((4, width), jnp.float32)
        for k in range(ITERS):
            hbr[k, 1] = jnp.zeros((n, 4, LANES), jnp.float32)
        for k in range(ITERS - 1):
            hsr[k, 1] = jnp.zeros((n, 4, LANES), jnp.float32)

    pl.semaphore_wait(barrier, greeted)
    announce_group()
    announce(0)

    halo_z(z0s.at[0], z0r.at[0], h_ss.at[0], h_rs.at[0])
    halo_y(y0s.at[0], y0r.at[0], h_ss.at[0, 2], h_rs.at[0, 2])
    halo_z(z0s.at[1], z0r.at[1], h_ss.at[1], h_rs.at[1])
    halo_y(y0s.at[1], y0r.at[1], h_ss.at[1, 2], h_rs.at[1, 2])

    reaction = lookup(0)
    cond_x = lookup(1)
    column = lax.broadcasted_iota(jnp.int32, (8, width), 1)
    xl = jnp.where(column >= 1, 0.5 * (cond_x + before(cond_x, 1)), 0.0)
    xu = jnp.where(column < width - 1, 0.5 * (cond_x + after(cond_x, 1)), 0.0)
    loads[3].wait()
    loads[4].wait()
    observed = merge(msk_v).astype(jnp.float32)
    counts = merge(cnt_v).astype(jnp.float32)
    growth = jnp.exp(latent)
    intensity = observed * growth

    arrived(y0r.at[0], h_rs.at[0, 2])
    halo_z_wait(z0r.at[0], h_rs.at[0])
    top = gy == 0
    bottom = gy == n - 1
    edge_y = rows_in(y0r.at[0, 0], y0r.at[0, 1])
    prev_y = jnp.where(is0, edge_y, up(cond_y, 1))
    next_y = jnp.where(is3, edge_y, down(cond_y, 1))
    yl = 0.5 * (cond_y + prev_y)
    yu = 0.5 * (cond_y + next_y)
    yl = jnp.where(is0 & top, 0.0, yl)
    yu = jnp.where(is3 & bottom, 0.0, yu)
    edge_z = merge(z0r.at[0])
    inner = 0.5 * (cond_z + up(cond_z, 4))
    outer = 0.5 * (cond_z + edge_z)
    closed = jnp.where(low, jnp.where(gz == 0, 1, 0), jnp.where(gz == m - 1, 1, 0)) == 1
    outer = jnp.where(closed, 0.0, outer)
    zl = jnp.where(low, outer, inner)
    zu = jnp.where(low, inner, outer)
    half = 0.5 * (reaction + intensity + (zl + zu))
    px = half + xl + xu
    py = half + yl + yu

    def put(name, values):
        coef[COEFS.index(name)] = values

    def get(name):
        return coef[COEFS.index(name)]

    def vput(name, values):
        vec[VECS.index(name)] = values

    def vget(name):
        return vec[VECS.index(name)]

    for name, values in (
        ("px", px), ("py", py), ("xl", xl), ("xu", xu), ("yl", yl), ("yu", yu),
        ("za", inner), ("zb", outer),
    ):
        put(name, values)

    d0 = spread(py, 0)
    d1 = spread(py, 1)
    d2 = spread(py, 2)
    a1 = spread(yl, 1)
    a2 = spread(yl, 2)
    l0 = spread(yl, 0)
    l3 = spread(yl, 3)
    minor0 = d1 * d2 - a2 * a2
    inv_det = 1.0 / (d0 * minor0 - a1 * a1 * d2)
    i00 = minor0 * inv_det
    i01 = a1 * d2 * inv_det
    i02 = a1 * a2 * inv_det
    i11 = d0 * d2 * inv_det
    i12 = a2 * d0 * inv_det
    i22 = (d0 * d1 - a1 * a1) * inv_det
    put("e0", jnp.where(is3, 1.0, l0 * i00))
    put("eu1", jnp.where(is3, l3 * i22, 0.0))
    put("eu2", jnp.where(is3, l3 * i12, 0.0))
    put("eu3", jnp.where(is3, l3 * i02, 0.0))
    put("ed1", jnp.where(is0, l0 * i01, 0.0))
    put("ed2", jnp.where(is0, l0 * i02, 0.0))
    put("g0", jnp.where(is0, i00, jnp.where(is1, i11, jnp.where(is2, i22, 0.0))))
    put("gd1", jnp.where(is0, i01, jnp.where(is1, i12, 0.0)))
    put("gd2", jnp.where(is0, i02, 0.0))
    put("gu1", jnp.where(is1, i01, jnp.where(is2, i12, 0.0)))
    put("gu2", jnp.where(is2, i02, 0.0))
    put("pp", l0 * jnp.where(is0, i00, jnp.where(is1, i01, jnp.where(is2, i02, 0.0))))
    put("qq", jnp.where(is3, 1.0, l3 * jnp.where(is0, i02, jnp.where(is1, i12, i22))))
    main = jnp.where(is3, py - l3 * l3 * i22, -(l0 * l0 * i00))
    link = jnp.where(is3, l3 * i02 * l0, 0.0)
    for chunk in range(n):
        block = pack(link, chunk)
        fs[chunk, 0:8] = pack(main, chunk)
        fs[chunk, 8:12] = jnp.where(
            sub1 == 0, down(block, 3), jnp.where(sub1 == 1, down(block, 4), jnp.where(sub1 == 2, down(block, 5), up(block, 2)))
        )[0:4]

    def exchange(src, dst, sems):
        dst[gy] = src[gy]
        for offset in far_first(n):
            target = peer("gy", offset)
            send(src.at[target], dst.at[gy], sems.at[0], sems.at[1], "gy", target)

    def received(dst, sems):
        arrived(dst.at[pl.ds(0, n - 1)], sems.at[1])

    pl.semaphore_wait(ready.at[0], 2)
    signal(ready.at[4], "gz", 1)
    signal(ready.at[4], "gz", m - 1)
    listen(0)
    announce(1)
    exchange(fs, fr, f_sem)
    for index, name in enumerate(("pp", "qq")):
        planes_out(get(name), cps.at[index])
        halo_z(cps.at[index], cpr.at[index], c_ss.at[index], c_rs.at[index])

    arrived(y0r.at[1], h_rs.at[1, 2])
    halo_z_wait(z0r.at[1], h_rs.at[1])
    edge_y = rows_in(y0r.at[1, 0], y0r.at[1, 1])
    edge_z = merge(z0r.at[1])
    center_q = reaction + xl + xu + yl + yu + zl + zu
    applied = (
        center_q * latent - xl * before(latent, 1) - xu * after(latent, 1)
        - yl * jnp.where(is0, edge_y, up(latent, 1))
        - yu * jnp.where(is3, edge_y, down(latent, 1))
        - inner * up(latent, 4) - outer * edge_z
    )
    rhs = observed * (counts - growth) - applied
    vput("r", rhs)

    def gather(values):
        return (
            get("e0") * values
            + get("eu1") * up(values, 1) + get("eu2") * up(values, 2) + get("eu3") * up(values, 3)
            + get("ed1") * down(values, 1) + get("ed2") * down(values, 2)
        )

    def forward(k, values):
        gathered = gather(values)
        for chunk in range(n):
            as_[k, chunk] = pack(gathered, chunk)
        exchange(as_.at[k], ar.at[k], a_sem.at[k])

    def x_factors():
        diagonal = get("px")
        band = get("xu")
        stride = 1
        level = 0
        while stride < width:
            inverse = 1.0 / diagonal
            scaled = band * inverse
            ahead = band * after(inverse, stride)
            wb[level] = before(scaled, stride)
            wa[level] = ahead
            diagonal = diagonal - before(scaled * band, stride) - ahead * band
            band = ahead * after(band, stride)
            stride = stride * 2
            level = level + 1
        xinv[...] = 1.0 / diagonal

    def solve_x(values):
        stride = 1
        level = 0
        while stride < width:
            values = values + wb[level] * before(values, stride) + wa[level] * after(values, stride)
            stride = stride * 2
            level = level + 1
        return values * xinv[...]

    def line_factors():
        received(fr, f_sem)
        inverse = None
        for i in range(n):
            diagonal = fr[i, 0:8]
            if i + 1 < n:
                diagonal = diagonal + up(fr[i + 1, 0:8], 3)
            diagonal = jnp.where(odd1, diagonal, 1.0)
            if i > 0:
                rows = fr[i, 8:12]
                rows = jnp.concatenate([rows, rows], axis=0)
                off = jnp.where(
                    sub1 == 3, up(rows, 3),
                    jnp.where(sub1 == 5, rows, jnp.where(sub1 == 7, up(rows, 1), up(rows, 2))),
                )
                off = jnp.where(odd1, off, 0.0)
                scale = off * inverse
                smul[i] = scale
                diagonal = diagonal - scale * off
            inverse = 1.0 / diagonal
            sinv[i] = inverse

    def correct(k, scale):
        halo_z_wait(hsr.at[k - 1], hs_rs.at[k - 1])
        if k == 1:
            received(kpr, kp_sem)
        for i in range(n):
            shares = []
            for first in (0, 2):
                quarter = [
                    jnp.broadcast_to(hsr[k - 1, side, i, first + part : first + part + 1], (8, LANES))
                    for side in range(2)
                    for part in range(2)
                ]
                shares.append(
                    jnp.where(
                        (sub1 == 0) | (sub1 == 3), quarter[0],
                        jnp.where(
                            (sub1 == 2) | (sub1 == 5), quarter[1],
                            jnp.where((sub1 == 4) | (sub1 == 7), quarter[2], quarter[3]),
                        ),
                    )
                )
            share = kpr[i, 0:8] * shares[0] + kpr[i, 8:16] * shares[1]
            corr[i] = -share if scale is None else scale * share

    def arrived_side(k, i):
        return ar[k, i] if k == 0 else ar[k, i] + corr[i]

    def solve_separators(k):
        received(ar.at[k], a_sem.at[k])
        carried = None
        for i in range(n):
            right = arrived_side(k, i)
            if i + 1 < n:
                right = right + up(arrived_side(k, i + 1), 3)
            carried = right if i == 0 else right + smul[i] * carried
            sol[i] = carried
        solved = None
        for i in range(n - 1, -1, -1):
            solved = sol[i] * sinv[i] if i == n - 1 else sol[i] * sinv[i] + smul[i + 1] * solved
            sol[i] = solved
        for i in range(n):
            below = sol[i - 1] if i > 0 else jnp.zeros((8, LANES), jnp.float32)
            block = jnp.where(odd1, sol[i], up(below, 5))
            bs[k, i] = block
            hbs[k, 0, i] = squeeze(block)
            hbs[k, 1, i] = squeeze(up(block, 4))
        if k == 0:
            pl.semaphore_wait(ready.at[4], 2)

        if k + 1 < ITERS:
            exchange(bs.at[k], br.at[k], b_sem.at[k])
            halo_z(hbs.at[k], hsr.at[k], hs_ss.at[k], hs_rs.at[k])

        @pl.when(has_prev)
        def _():
            for offset in far_first(n) + [0]:
                target = peer("gy", offset)
                send_diagonal(
                    hbs.at[k, 0, target], hbr.at[k, 1, gy], hb_ss.at[k, 0], hb_rs.at[k, 1],
                    target, peer("gz", m - 1),
                )

        @pl.when(has_next)
        def _():
            for offset in far_first(n) + [0]:
                target = peer("gy", offset)
                send_diagonal(
                    hbs.at[k, 1, target], hbr.at[k, 0, gy], hb_ss.at[k, 1], hb_rs.at[k, 0],
                    target, peer("gz", 1),
                )

        if k + 1 == ITERS:
            exchange(bs.at[k], br.at[k], b_sem.at[k])

    def squeeze(block):
        return jnp.where(sub1 == 0, block, jnp.where(sub1 == 3, down(block, 2), down(block, 1)))[0:4]

    def unpack_halo(k, first):
        parts = []
        for chunk in range(n):
            for part in range(2):
                pair = [
                    jnp.broadcast_to(hbr[k, side, chunk, first + part : first + part + 1], (8, LANES))
                    for side in range(2)
                ]
                parts.append(jnp.where(sub1 < 4, pair[0], pair[1]))
        return jnp.concatenate(parts, axis=1)

    def unpack(k):
        parts = []
        for chunk in range(n):
            block = br[k, chunk]
            parts += [block, up(block, 6)]
        return jnp.concatenate(parts, axis=1)

    def apply_pair(k, name, middle, extra=None, scale=None):
        values = vget(name)
        forward(k, values)
        if k == 0:
            x_factors()
        if extra is not None:
            extra()
        along_x = solve_x(vget(name))
        vput("ax", along_x)
        rows_out(along_x, ys.at[k])
        halo_y(ys.at[k], yr.at[k], k_ss.at[k, 2], k_rs.at[k, 2])
        if k == 0:
            line_factors()
        values = vget(name)
        inner_y = (
            get("g0") * values + get("gu1") * up(values, 1) + get("gu2") * up(values, 2)
            + get("gd1") * down(values, 1) + get("gd2") * down(values, 2)
        )
        vput("ay", inner_y)
        planes_out(vget("ax") + inner_y, zs.at[k])
        halo_z(zs.at[k], zr.at[k], k_ss.at[k], k_rs.at[k])
        if k > 0:
            correct(k, scale)
        solve_separators(k)
        if k == 0:
            listen(1)
            announce(2)
            for index in range(2):
                halo_z_wait(cpr.at[index], c_rs.at[index])
                put(("hp", "hq")[index], get("zb") * merge(cpr.at[index]))
            for index, name_h in enumerate(("hp", "hq")):
                gathered = gather(get(name_h))
                for chunk in range(n):
                    kps[chunk, 8 * index : 8 * index + 8] = pack(gathered, chunk)
            exchange(kps, kpr, kp_sem)
        if middle is not None:
            middle()
        arrived(yr.at[k], k_rs.at[k, 2])
        along_x = vget("ax")
        edge = rows_in(yr.at[k, 0], yr.at[k, 1])
        halo_z_wait(zr.at[k], k_rs.at[k])
        vput(
            "part",
            2.0 * vget(name) + get("py") * along_x
            - get("yl") * jnp.where(is0, edge, up(along_x, 1))
            - get("yu") * jnp.where(is3, edge, down(along_x, 1))
            - get("zb") * merge(zr.at[k]),
        )
        received(br.at[k], b_sem.at[k])
        ends = unpack(k)
        along_y = vget("ay") + get("pp") * spread(ends, 0) + get("qq") * spread(ends, 3)
        total = vget("ax") + along_y
        image = (
            vget("part") + get("px") * along_y
            - get("xl") * before(along_y, 1) - get("xu") * after(along_y, 1)
            - get("za") * up(total, 4)
        )
        return total, image

    def halo_share(k):
        halo_z_wait(hbr.at[k], hb_rs.at[k])
        return get("hp") * unpack_halo(k, 0) + get("hq") * unpack_halo(k, 2)

    def fold(first, second):
        product = first * second
        acc = product[:, 0:LANES]
        for t in range(1, tiles):
            acc = acc + product[:, t * LANES : (t + 1) * LANES]
        return jnp.sum(jnp.sum(acc, axis=0, keepdims=True), axis=1, keepdims=True)

    lane = lax.broadcasted_iota(jnp.int32, (1, LANES), 1)

    def reduce_start(k, sums):
        packed = jnp.zeros((1, LANES), jnp.float32)
        for index, value in enumerate(sums):
            packed = jnp.where(lane == index, value, packed)
        p1s[k] = packed
        p1r[k, gy] = packed
        for offset in far_first(n):
            send(p1s.at[k], p1r.at[k, gy], p1_sem.at[k, 0], p1_sem.at[k, 1], "gy", peer("gy", offset))

    def reduce_middle(k):
        arrived(p1r.at[k, pl.ds(0, n - 1)], p1_sem.at[k, 1])
        total = p1r[k, 0]
        for i in range(1, n):
            total = total + p1r[k, i]
        p2s[k] = total
        p2r[k, gz] = total
        for offset in hops_first(m):
            send(p2s.at[k], p2r.at[k, gz], p2_sem.at[k, 0], p2_sem.at[k, 1], "gz", peer("gz", offset))

    def reduce_end(k, count):
        arrived(p2r.at[k, pl.ds(0, m - 1)], p2_sem.at[k, 1])
        total = p2r[k, 0]
        for i in range(1, m):
            total = total + p2r[k, i]
        return [total[:, index : index + 1] for index in range(count)]

    u0, w0 = apply_pair(0, "r", None)
    vput("u0", u0)
    vput("w0", w0)

    listen(2)

    def start0():
        vput("w0", vget("w0") - halo_share(0))
        reduce_start(0, (fold(vget("r"), vget("u0")), fold(vget("u0"), vget("w0"))))

    def middle0():
        reduce_middle(0)

    q0, z0 = apply_pair(1, "w0", middle0, start0)
    vput("q0", q0)
    vput("z0", z0)
    g0, e0 = reduce_end(0, 2)
    alpha0 = g0 / e0
    r1 = vget("r") - alpha0 * vget("w0")
    u1 = vget("u0") - alpha0 * vget("q0")
    w1 = vget("w0") - alpha0 * vget("z0")
    vput("r", r1)
    vput("u1", u1)
    vput("w1", w1)

    def start1():
        share = halo_share(1)
        vput("z0", vget("z0") - share)
        vput("w1", vget("w1") + alpha0 * share)
        reduce_start(
            1,
            (
                fold(vget("r"), vget("u1")),
                fold(vget("u1"), vget("w1")),
                fold(vget("u1"), vget("w0")),
            ),
        )

    def middle1():
        reduce_middle(1)

    q1, z1 = apply_pair(2, "w1", middle1, start1, alpha0)
    g1, uw1, c1 = reduce_end(1, 3)
    beta1 = g1 / g0
    e1 = uw1 + 2.0 * beta1 * c1 + beta1 * beta1 * e0
    alpha1 = g1 / e1
    s1 = vget("w1") + beta1 * vget("w0")
    r2 = vget("r") - alpha1 * s1
    u2 = vget("u1") - alpha1 * (q1 + beta1 * vget("q0"))
    w2 = vget("w1") - alpha1 * (z1 + beta1 * vget("z0"))
    sums = (fold(r2, u2), fold(u2, w2), fold(u2, s1))
    vput("u1", vget("u1") + beta1 * vget("u0"))
    vput("r", u2)
    share = halo_share(2)
    reduce_start(2, (sums[0], sums[1] + alpha1 * fold(vget("r"), share), sums[2]))
    reduce_middle(2)
    dir1 = vget("u1")
    done = alpha0 * vget("u0") + alpha1 * dir1
    g2, uw2, c2 = reduce_end(2, 3)
    beta2 = g2 / g1
    e2 = uw2 + 2.0 * beta2 * c2 + beta2 * beta2 * e1
    alpha2 = g2 / e2
    result = done + alpha2 * (vget("r") + beta2 * dir1)
    out[0] = result[0:4]
    out[1] = result[4:8]
    for index in range(2):
        halo_z_sent(z0s.at[index], h_ss.at[index])
        arrived(y0s.at[index], h_ss.at[index, 2])
        halo_z_sent(cps.at[index], c_ss.at[index])
    for k in range(ITERS - 1):
        halo_z_sent(hbs.at[k], hs_ss.at[k])
    arrived(kps.at[pl.ds(0, n - 1)], kp_sem.at[0])
    arrived(fs.at[pl.ds(0, n - 1)], f_sem.at[0])
    for k in range(ITERS):
        arrived(as_.at[k, pl.ds(0, n - 1)], a_sem.at[k, 0])
        arrived(bs.at[k, pl.ds(0, n - 1)], b_sem.at[k, 0])
        halo_z_sent(zs.at[k], k_ss.at[k])
        halo_z_sent(hbs.at[k], hb_ss.at[k])
        arrived(ys.at[k], k_ss.at[k, 2])
        arrived(p1r.at[k, pl.ds(0, n - 1)], p1_sem.at[k, 0])
        arrived(p2r.at[k, pl.ds(0, m - 1)], p2_sem.at[k, 0])


def shards(latent, event_counts, survey_mask, class_ids, class_table):
    planes, rows, width = latent.shape
    n = lax.axis_size("gy")
    m = lax.axis_size("gz")
    assert planes == 2 and rows == 4 and width == n * 2 * LANES
    levels = 0
    while (1 << levels) < width:
        levels = levels + 1
    f32 = jnp.float32
    dma = pltpu.SemaphoreType.DMA
    vmem = pltpu.VMEM
    block = (2, 4, width)
    scratch = [
        vmem(block, f32), vmem(block, jnp.int32), vmem(block, jnp.int32), vmem(block, jnp.int32),
        pltpu.SMEM(class_table.shape, f32), dma((5,)), pltpu.SemaphoreType.REGULAR((5,)),
        vmem((2, 2, 2, width), f32), vmem((2, 2, 2, width), f32),
        vmem((2, 2, 4, width), f32), vmem((2, 2, 4, width), f32), dma((2, 3)), dma((2, 3)),
        vmem((n, 12, LANES), f32), vmem((n, 12, LANES), f32), dma((2,)),
        vmem((3, n, 8, LANES), f32), vmem((3, n, 8, LANES), f32), dma((3, 2)),
        vmem((3, n, 8, LANES), f32), vmem((3, n, 8, LANES), f32), dma((3, 2)),
        vmem((3, 2, 2, width), f32), vmem((3, 2, 2, width), f32),
        vmem((3, 2, 4, width), f32), vmem((3, 2, 4, width), f32), dma((3, 3)), dma((3, 3)),
        vmem((3, 2, n, 4, LANES), f32), vmem((3, 2, n, 4, LANES), f32), dma((3, 2)), dma((3, 2)),
        vmem((2, 2, n, 4, LANES), f32), dma((2, 2)), dma((2, 2)),
        vmem((n, 16, LANES), f32), vmem((n, 16, LANES), f32), dma((2,)),
        vmem((2, 2, 4, width), f32), vmem((2, 2, 4, width), f32), dma((2, 2)), dma((2, 2)),
        vmem((3, 1, LANES), f32), vmem((3, n, 1, LANES), f32), dma((3, 2)),
        vmem((3, 1, LANES), f32), vmem((3, m, 1, LANES), f32), dma((3, 2)),
        vmem((levels, 8, width), f32), vmem((levels, 8, width), f32), vmem((8, width), f32),
        vmem((len(COEFS), 8, width), f32), vmem((len(VECS), 8, width), f32),
        vmem((n, 8, LANES), f32), vmem((n, 8, LANES), f32), vmem((n, 8, LANES), f32),
        vmem((n, 8, LANES), f32),
    ]
    anywhere = pl.BlockSpec(memory_space=pl.ANY)
    return pl.pallas_call(
        functools.partial(kernel, n, m, width),
        out_shape=pltpu.VMEM(block, f32),
        in_specs=[anywhere] * 5,
        out_specs=pl.BlockSpec(memory_space=pltpu.VMEM),
        scratch_shapes=scratch,
        compiler_params=pltpu.CompilerParams(collective_id=0, has_side_effects=True),
        name="newton",
    )(latent, event_counts, survey_mask, class_ids, class_table)


def solution(mesh):
    placed = (
        P("gz", "gy", None),
        P("gz", "gy", None),
        P("gz", "gy", None),
        P("gz", "gy", None),
        P(),
    )
    return jax.shard_map(
        shards, mesh=mesh, in_specs=placed, out_specs=P("gz", "gy", None), check_vma=False
    )
```
